768 devices in a mesh: branch: 2 (over y_lo), hidden: 48 (over x, z), width: 8 (over y_hi, core).
Axes of the slice: x: 4, y: 8 (y_hi: 4, y_lo: 2; y = y_hi * 2 + y_lo), z: 12, core: 2. Of those that a mesh axis runs over, the one named last changes fastest.
Arguments:
- rows: bfloat16 [2, 288, 4096], P(None, ('branch', 'hidden'), 'width'), may hold values from -6 to 6
- cotangent: bfloat16 [2, 288, 4096], P(None, ('branch', 'hidden'), 'width'), may hold values from -6 to 6
- labels: int32 [2, 288], P(None, ('branch', 'hidden')), may hold values from 0 to 1, as said below
- counts: int32 [2, 96], P(None, ('branch', 'hidden')), may hold values from 1 to 3, as said below
- gate_weight: bfloat16 [2, 4096, 12288], P('branch', 'width', 'hidden'), may hold values from -0.09375 to 0.09375
- up_weight: bfloat16 [2, 4096, 12288], P('branch', 'width', 'hidden'), may hold values from -0.09375 to 0.09375
- down_weight: bfloat16 [2, 12288, 4096], P('branch', 'hidden', 'width'), may hold values from -0.0546875 to 0.0546875
Outputs:
- output: bfloat16 [2, 288, 4096], P(None, ('branch', 'hidden'), 'width')
- grad_rows: bfloat16 [2, 288, 4096], P(None, ('branch', 'hidden'), 'width')
- grad_gate: float32 [2, 4096, 12288], P('branch', 'width', 'hidden')
- grad_up: float32 [2, 4096, 12288], P('branch', 'width', 'hidden')
- grad_down: float32 [2, 12288, 4096], P('branch', 'hidden', 'width')
The draws below stay inside these ranges and needn't reach their ends.
Inputs may be any that keep to these rules, and one draw needn't show every extreme that they name: The first counts rows of an owner are used; one owner in each microbatch uses all 3. `labels`: among the used rows of one owner in one microbatch at most 2 carry the same label; some owner in each microbatch has exactly 2 text rows.
All inputs are finite; a program needn't handle non-finite values.
Results may differ from the reference program's by a relative error of at most 0.0049.
Values may be sent and summed in bfloat16 or wider, within the bound.
No kernel may reach another device: no remote copies, remote signals or barrier semaphores. Data moves between devices by JAX's collectives and lax.ppermute only.
A program may use at most 32 MiB of HBM per device.

```python
import jax
import jax.numpy as jnp

D = 4096
FF = 12288
MB = 2
ROW_DEV = 3
CAP = 2
GROUPS = 96
ROWS = 288


def routing_draw(key):
    base = jax.random.fold_in(key, 7)
    key_count, key_pick, key_order = jax.random.split(base, 3)
    used = jax.random.randint(key_count, (MB, GROUPS), ROW_DEV // 3, ROW_DEV + 1)
    used = used.at[:, 0].set(ROW_DEV)
    lowest = jnp.maximum(0, used - CAP)
    highest = jnp.minimum(used, CAP)
    picked = jax.random.randint(key_pick, (MB, GROUPS), 0, 1 << 20)
    text_rows = lowest + picked % (highest - lowest + 1)
    text_rows = text_rows.at[:, 0].set(CAP)
    position = jnp.arange(ROW_DEV, dtype=jnp.int32)
    scores = jax.random.randint(key_order, (MB, GROUPS, ROW_DEV), 0, 1 << 16) * ROW_DEV + position
    scores = jnp.where(position >= used[:, :, None], scores + (1 << 22), scores)
    ranking = jnp.argsort(jnp.argsort(scores, axis=-1, stable=True), axis=-1, stable=True)
    labels = (ranking >= text_rows[:, :, None]).astype(jnp.int32)
    return (used.astype(jnp.int32), labels.reshape(MB, GROUPS * ROW_DEV))


def draw_labels(key, part):
    return routing_draw(key)[1]


def draw_counts(key, part):
    return routing_draw(key)[0]


def shard_levels(own_key, shape, shards, smallest, largest):
    level = 1.0
    for dim, parts in shards:
        steps = jax.random.uniform(jax.random.fold_in(jax.random.fold_in(own_key, 6), dim), (parts,), jnp.float32, smallest / len(shards), largest / len(shards))
        level = level * jnp.repeat(jnp.exp(steps), shape[dim] // parts).reshape((-1,) + (1,) * (len(shape) - 1 - dim))
    return level


def bell_draw(own_key, extent, width, bound, shards=(), kind=jnp.bfloat16):
    level = shard_levels(own_key, extent, shards, -0.22, 0.18) if shards else 1.0
    drawn = jax.random.normal(own_key, extent, jnp.float32) * width * level
    return jnp.minimum(jnp.maximum(drawn, -bound), bound).astype(kind)


def setup_inputs(seed: int = 0) -> dict:
    key_list = jax.random.split(jax.random.key(seed), 8)
    return {
        "rows": bell_draw(key_list[0], (MB, ROWS, D), 1.0, 6.0, ((1, 96), (2, 8))),
        "cotangent": bell_draw(key_list[1], (MB, ROWS, D), 1.0, 6.0, ((1, 96), (2, 8))),
        "labels": draw_labels(jax.random.fold_in(key_list[7], 71), 0),
        "counts": draw_counts(jax.random.fold_in(key_list[7], 71), 0),
        "gate_weight": bell_draw(key_list[4], (2, D, FF), D ** -0.5, 0.09375, ((0, 2), (1, 8), (2, 48))),
        "up_weight": bell_draw(key_list[5], (2, D, FF), D ** -0.5, 0.09375, ((0, 2), (1, 8), (2, 48))),
        "down_weight": bell_draw(key_list[6], (2, FF, D), FF ** -0.5, 0.0546875, ((0, 2), (1, 48), (2, 8))),
    }


def reference(rows, cotangent, labels, counts, gate_weight, up_weight, down_weight):
    position = jnp.arange(ROWS, dtype=jnp.int32) % ROW_DEV
    outputs = []
    row_grads = []
    grad_gate = [jnp.zeros((D, FF), jnp.float32) for branch in range(2)]
    grad_up = [jnp.zeros((D, FF), jnp.float32) for branch in range(2)]
    grad_down = [jnp.zeros((FF, D), jnp.float32) for branch in range(2)]
    for micro in range(MB):
        valid = position < jnp.repeat(counts[micro], ROW_DEV)
        inputs = rows[micro]
        upstream = cotangent[micro]
        output = jnp.zeros((ROWS, D), jnp.bfloat16)
        back_rows = jnp.zeros((ROWS, D), jnp.bfloat16)
        for branch in range(2):
            chosen = (valid & (labels[micro] == branch))[:, None]
            gate = jnp.dot(inputs, gate_weight[branch], preferred_element_type=jnp.float32)
            up_value = jnp.dot(inputs, up_weight[branch], preferred_element_type=jnp.float32)
            sigma = jax.nn.sigmoid(gate)
            silu = gate * sigma
            hidden = (silu * up_value).astype(jnp.bfloat16)
            result = jnp.dot(hidden, down_weight[branch], preferred_element_type=jnp.float32).astype(jnp.bfloat16)
            output = jnp.where(chosen, result, output)
            masked = jnp.where(chosen, upstream, jnp.zeros_like(upstream))
            dhid = jnp.dot(masked, down_weight[branch].T, preferred_element_type=jnp.float32)
            dgate = (dhid * up_value * sigma * (1.0 + gate * (1.0 - sigma))).astype(jnp.bfloat16)
            dup = (dhid * silu).astype(jnp.bfloat16)
            back = (jnp.dot(dgate, gate_weight[branch].T, preferred_element_type=jnp.float32)
                    + jnp.dot(dup, up_weight[branch].T, preferred_element_type=jnp.float32)).astype(jnp.bfloat16)
            back_rows = jnp.where(chosen, back, back_rows)
            grad_gate[branch] = grad_gate[branch] + jnp.dot(inputs.T, dgate, preferred_element_type=jnp.float32)
            grad_up[branch] = grad_up[branch] + jnp.dot(inputs.T, dup, preferred_element_type=jnp.float32)
            grad_down[branch] = grad_down[branch] + jnp.dot(hidden.T, masked, preferred_element_type=jnp.float32)
        outputs.append(output)
        row_grads.append(back_rows)
    return (jnp.stack(outputs), jnp.stack(row_grads), jnp.stack(grad_gate),
            jnp.stack(grad_up), jnp.stack(grad_down))
```

```python
import jax
import jax.numpy as jnp
from jax import lax
from jax.sharding import PartitionSpec as P

CAP = 2
BF16 = jnp.bfloat16
F32 = jnp.float32
OWNERS = ("branch", "hidden")


def slot_masks(labels, counts):
    masks = []
    for branch in (0, 1):
        chosen = [
            (counts[:, 0:1] > p) & (labels[:, p : p + 1] == branch)
            for p in range(labels.shape[1])
        ]
        slots = []
        for s in range(CAP):
            picks = []
            for p in range(labels.shape[1]):
                rank = sum((c.astype(jnp.int32) for c in chosen[:p]), jnp.int32(0))
                picks.append(chosen[p] & (rank == s))
            slots.append(picks)
        masks.append(slots)
    return masks


def contract(left, right, left_dim, right_dim):
    return lax.dot_general(
        left, right, (((left_dim,), (right_dim,)), ((), ())), preferred_element_type=F32
    )


def shards(rows, cotangent, labels, counts, gate_weight, up_weight, down_weight):
    gate_weight, up_weight, down_weight = gate_weight[0], up_weight[0], down_weight[0]
    mb, row_dev, width_part = rows.shape
    hidden_size = lax.axis_size("hidden")
    width_size = lax.axis_size("width")
    owners = 2 * hidden_size
    per_owner = mb * CAP
    slots = owners * per_owner
    units = gate_weight.shape[1]
    masks = slot_masks(labels, counts)

    zero = jnp.zeros((), BF16)
    packed = []
    for branch in (0, 1):
        for source in (rows, cotangent):
            for s in range(CAP):
                value = zero
                for p in range(row_dev):
                    value = jnp.where(masks[branch][s][p], source[:, p, :], value)
                packed.append(value)
    packed = jnp.stack(packed).reshape(2, 1, 2 * CAP * mb, width_part)
    send = jnp.broadcast_to(packed, (2, hidden_size, 2 * CAP * mb, width_part))
    recv = lax.all_to_all(
        send.reshape(owners, 2 * per_owner, width_part), OWNERS, 0, 0, tiled=True
    )
    flat_rows = recv[:, :per_owner].reshape(slots, width_part)
    flat_cot = recv[:, per_owner:].reshape(slots, width_part)

    parts = jnp.stack(
        [
            contract(gate_weight, flat_rows, 0, 1),
            contract(up_weight, flat_rows, 0, 1),
            contract(down_weight, flat_cot, 1, 1),
        ]
    ).astype(BF16)
    parts = parts.reshape(3, width_size, units // width_size, slots).transpose(1, 0, 2, 3)
    parts = lax.all_to_all(parts, "width", 0, 0, tiled=True)
    gate, up_value, dhid = jnp.sum(parts.astype(F32), axis=0)
    sigma = jax.nn.sigmoid(gate)
    silu = gate * sigma
    share = jnp.stack(
        [
            (silu * up_value).astype(BF16),
            (dhid * up_value * sigma * (1.0 + gate * (1.0 - sigma))).astype(BF16),
            (dhid * silu).astype(BF16),
        ]
    )
    every = lax.all_gather(share, "width", axis=0, tiled=False)
    hidden = every[:, 0].reshape(units, slots)
    dgate = every[:, 1].reshape(units, slots)
    dup = every[:, 2].reshape(units, slots)

    out_part = contract(hidden, down_weight, 0, 0)
    back_part = contract(dgate, gate_weight, 0, 1) + contract(dup, up_weight, 0, 1)
    result = jnp.stack(
        [
            out_part.astype(BF16).reshape(owners, per_owner, width_part),
            back_part.astype(BF16).reshape(owners, per_owner, width_part),
        ],
        axis=1,
    ).reshape(owners, 2 * per_owner, width_part)
    result = lax.all_to_all(result, OWNERS, 0, 0, tiled=True)
    grad_gate = contract(flat_rows, dgate, 0, 1)
    grad_up = contract(flat_rows, dup, 0, 1)
    grad_down = contract(hidden, flat_cot, 1, 0)
    result = jnp.sum(
        result.reshape(2, hidden_size, 2, CAP, mb, width_part).astype(F32), axis=1
    )
    result = lax.optimization_barrier(result).astype(BF16)
    finals = []
    for which in (0, 1):
        per_row = []
        for p in range(row_dev):
            value = zero
            for branch in (0, 1):
                for s in range(CAP):
                    value = jnp.where(masks[branch][s][p], result[branch, which, s], value)
            per_row.append(value)
        finals.append(jnp.stack(per_row, axis=1))
    return (finals[0], finals[1], grad_gate[None], grad_up[None], grad_down[None])


def solution(mesh):
    owner_rows = P(None, OWNERS, "width")
    return jax.shard_map(
        shards,
        mesh=mesh,
        in_specs=(
            owner_rows,
            owner_rows,
            P(None, OWNERS),
            P(None, OWNERS),
            P("branch", "width", "hidden"),
            P("branch", "width", "hidden"),
            P("branch", "hidden", "width"),
        ),
        out_specs=(
            owner_rows,
            owner_rows,
            P("branch", "width", "hidden"),
            P("branch", "width", "hidden"),
            P("branch", "hidden", "width"),
        ),
        check_vma=False,
    )
```

```python
import jax
import jax.numpy as jnp
from jax import lax
from jax.sharding import Mesh, PartitionSpec as P

CAP = 2
BF16 = jnp.bfloat16
F32 = jnp.float32
SUB = (4, 12, 4, 2)
NAMES = ("branch", "hidden_x", "hidden_z", "width_y", "width_core")
HIDDEN = ("hidden_x", "hidden_z")
WIDTH = ("width_y", "width_core")
OWNERS = ("branch",) + HIDDEN
NEAR = ("branch", "hidden_z")


def slot_table(labels, counts):
    mb, row_dev = labels.shape
    shape = (2, mb, row_dev, row_dev)
    branch, _, here, other = (lax.broadcasted_iota(jnp.int32, shape, d) for d in range(4))
    counted = (other < counts[None, :, :, None]) & (labels[None, :, None, :] == branch)
    rank = jnp.sum(jnp.where(counted & (other < here), 1, 0), axis=3)
    own = jnp.sum(jnp.where(counted & (other == here), 1, 0), axis=3)
    rank = jnp.where(own == 1, rank, -1)
    slot = lax.broadcasted_iota(jnp.int32, (2, CAP, mb, row_dev), 1)
    return rank[:, None] == slot


def contract(left, right, left_dim, right_dim):
    return lax.dot_general(
        left, right, (((left_dim,), (right_dim,)), ((), ())), preferred_element_type=F32
    )


def own_kept(own, received, axis):
    place = lax.broadcasted_iota(jnp.int32, own.shape, 0)
    mine = place == lax.axis_index(axis)
    return jnp.sum(jnp.where(mine, own, received.astype(F32)), axis=0)


def shards(rows, cotangent, labels, counts, gate_weight, up_weight, down_weight):
    gate_weight, up_weight, down_weight = gate_weight[0], up_weight[0], down_weight[0]
    mb, row_dev, width = rows.shape
    size_x, size_z = lax.axis_size("hidden_x"), lax.axis_size("hidden_z")
    size_y, size_c = lax.axis_size("width_y"), lax.axis_size("width_core")
    near = 2 * size_z
    per_owner = mb * CAP
    block = near * per_owner
    slots = size_x * block
    units = gate_weight.shape[1]
    share_units = units // (size_y * size_c)
    table = slot_table(labels, counts)

    source = jnp.stack([rows, cotangent])
    packed = jnp.sum(
        jnp.where(
            table[:, None, :, :, :, None], source[None, :, None].astype(F32), 0.0
        ),
        axis=4,
    ).astype(BF16)
    packed = packed.reshape(2, 1, 2 * per_owner, width)
    send = jnp.broadcast_to(packed, (2, size_z, 2 * per_owner, width))
    recv = lax.all_to_all(
        send.reshape(near, 2 * per_owner, width), NEAR, 0, 0, tiled=True
    )
    recv = recv.reshape(near, 2, per_owner, width).transpose(1, 0, 2, 3)
    every = lax.all_gather(recv.reshape(2, block, width), "hidden_x", axis=0, tiled=False)
    flat_rows = every[:, 0].reshape(slots, width)
    flat_cot = every[:, 1].reshape(slots, width)

    parts = jnp.stack(
        [
            contract(gate_weight, flat_rows, 0, 1),
            contract(up_weight, flat_rows, 0, 1),
            contract(down_weight, flat_cot, 1, 1),
        ]
    )
    parts = parts.reshape(3, size_y, size_c, share_units, slots).transpose(2, 1, 0, 3, 4)
    pair = lax.all_to_all(parts, "width_core", 0, 0, tiled=True)
    pair = pair[0] + pair[1]
    sent = lax.all_to_all(pair.astype(BF16), "width_y", 0, 0, tiled=True)
    gate, up_value, dhid = own_kept(pair, sent, "width_y")
    sigma = jax.nn.sigmoid(gate)
    silu = gate * sigma
    share = jnp.stack(
        [
            (silu * up_value).astype(BF16),
            (dhid * up_value * sigma * (1.0 + gate * (1.0 - sigma))).astype(BF16),
            (dhid * silu).astype(BF16),
        ]
    )
    acts = lax.all_gather(share, WIDTH, axis=0, tiled=False)
    hidden = acts[:, 0].reshape(units, slots)
    dgate = acts[:, 1].reshape(units, slots)
    dup = acts[:, 2].reshape(units, slots)

    out_part = contract(hidden, down_weight, 0, 0)
    back_part = contract(dgate, gate_weight, 0, 1) + contract(dup, up_weight, 0, 1)
    result = jnp.stack(
        [out_part.reshape(size_x, block, width), back_part.reshape(size_x, block, width)],
        axis=1,
    )
    sent = lax.all_to_all(result.astype(BF16), "hidden_x", 0, 0, tiled=True)
    grad_gate = contract(flat_rows, dgate, 0, 1)
    grad_up = contract(flat_rows, dup, 0, 1)
    grad_down = contract(hidden, flat_cot, 1, 0)
    result = own_kept(result, sent, "hidden_x").astype(BF16)
    result = result.reshape(2, near, per_owner, width).transpose(1, 0, 2, 3)
    result = lax.all_to_all(
        result.reshape(near, 2 * per_owner, width), NEAR, 0, 0, tiled=True
    )
    result = jnp.sum(
        result.reshape(2, size_z, 2, CAP, mb, width).astype(F32), axis=1
    )
    result = lax.optimization_barrier(result).astype(BF16)
    finals = []
    for which in (0, 1):
        per_row = []
        for p in range(row_dev):
            value = jnp.zeros((), BF16)
            for branch in (0, 1):
                for s in range(CAP):
                    value = jnp.where(
                        table[branch, s, :, p : p + 1], result[branch, which, s], value
                    )
            per_row.append(value)
        finals.append(jnp.stack(per_row, axis=1))
    return (finals[0], finals[1], grad_gate[None], grad_up[None], grad_down[None])


def solution(mesh):
    mesh = Mesh(mesh.devices.reshape((2,) + SUB), NAMES)
    owner_rows = P(None, OWNERS, WIDTH)
    return jax.shard_map(
        shards,
        mesh=mesh,
        in_specs=(
            owner_rows,
            owner_rows,
            P(None, OWNERS),
            P(None, OWNERS),
            P("branch", WIDTH, HIDDEN),
            P("branch", WIDTH, HIDDEN),
            P("branch", HIDDEN, WIDTH),
        ),
        out_specs=(
            owner_rows,
            owner_rows,
            P("branch", WIDTH, HIDDEN),
            P("branch", WIDTH, HIDDEN),
            P("branch", HIDDEN, WIDTH),
        ),
        check_vma=False,
    )
```

```python
import jax
import jax.numpy as jnp
from jax import lax
from jax.experimental import pallas as pl
from jax.experimental.layout import Layout, with_layout_constraint
from jax.experimental.pallas import tpu as pltpu
from jax.sharding import Mesh, PartitionSpec as P

CAP = 2
BF16 = jnp.bfloat16
F32 = jnp.float32
SUB = (4, 12, 4, 2)
NAMES = ("branch", "hidden_x", "hidden_z", "width_y", "width_core")
HIDDEN = ("hidden_x", "hidden_z")
WIDTH = ("width_y", "width_core")
OWNERS = ("branch",) + HIDDEN
NEAR = ("branch", "hidden_z")


def slot_table(labels, counts):
    mb, row_dev = labels.shape
    shape = (2, mb, row_dev, row_dev)
    branch, _, here, other = (lax.broadcasted_iota(jnp.int32, shape, d) for d in range(4))
    counted = (other < counts[None, :, :, None]) & (labels[None, :, None, :] == branch)
    rank = jnp.sum(jnp.where(counted & (other < here), 1, 0), axis=3)
    own = jnp.sum(jnp.where(counted & (other == here), 1, 0), axis=3)
    rank = jnp.where(own == 1, rank, -1)
    slot = lax.broadcasted_iota(jnp.int32, (2, CAP, mb, row_dev), 1)
    return rank[:, None] == slot


def contract(left, right, left_dim, right_dim):
    return lax.dot_general(
        left, right, (((left_dim,), (right_dim,)), ((), ())), preferred_element_type=F32
    )


def own_kept(own, received, axis):
    place = lax.broadcasted_iota(jnp.int32, own.shape, 0)
    mine = place == lax.axis_index(axis)
    return jnp.sum(jnp.where(mine, own, received.astype(F32)), axis=0)


def full(shape):
    return pl.BlockSpec(shape, lambda: (0,) * len(shape))


def second_kernel(place_ref, acts_ref, gate_ref, up_ref, down_ref, sent_ref, own_ref, scratch):
    parts, kinds, share_units, slots = acts_ref.shape
    units = parts * share_units
    width = down_ref.shape[1]
    hidden = acts_ref[:, 0].reshape(units, slots)
    dgate = acts_ref[:, 1].reshape(units, slots)
    dup = acts_ref[:, 2].reshape(units, slots)
    out = contract(hidden, down_ref[...], 0, 0)
    back = contract(dgate, gate_ref[...], 0, 1) + contract(dup, up_ref[...], 0, 1)
    tiles = slots // 8
    out = out.reshape(tiles, 8, width)
    back = back.reshape(tiles, 8, width)
    first = lax.broadcasted_iota(jnp.int32, out.shape, 1) < 4
    even = jnp.where(first, out, pltpu.roll(back, 4, 1))
    odd = jnp.where(first, pltpu.roll(out, 4, 1), back)
    sent_ref[:, 0] = even.astype(BF16)
    sent_ref[:, 1] = odd.astype(BF16)
    scratch[:, 0] = even
    scratch[:, 1] = odd
    own_tiles = own_ref.shape[0]
    own_ref[...] = scratch[pl.ds(place_ref[0] * own_tiles, own_tiles)]


def second_products(place, acts, gate_weight, up_weight, down_weight, size_x):
    slots = acts.shape[3]
    width = down_weight.shape[1]
    shape = (slots // 8, 2, 8, width)
    own_shape = (slots // 8 // size_x, 2, 8, width)
    return pl.pallas_call(
        second_kernel,
        out_shape=(
            jax.ShapeDtypeStruct(shape, BF16),
            jax.ShapeDtypeStruct(own_shape, F32),
        ),
        in_specs=[
            pl.BlockSpec(memory_space=pltpu.SMEM),
            full(acts.shape),
            full(gate_weight.shape),
            full(up_weight.shape),
            full(down_weight.shape),
        ],
        out_specs=(full(shape), full(own_shape)),
        scratch_shapes=[pltpu.VMEM(shape, F32)],
        name="second_products",
    )(place, acts, gate_weight, up_weight, down_weight)


def shards(rows, cotangent, labels, counts, gate_weight, up_weight, down_weight):
    gate_weight, up_weight, down_weight = gate_weight[0], up_weight[0], down_weight[0]
    mb, row_dev, width = rows.shape
    size_x, size_z = lax.axis_size("hidden_x"), lax.axis_size("hidden_z")
    size_y, size_c = lax.axis_size("width_y"), lax.axis_size("width_core")
    near = 2 * size_z
    per_owner = mb * CAP
    block = near * per_owner
    slots = size_x * block
    units = gate_weight.shape[1]
    share_units = units // (size_y * size_c)
    table = slot_table(labels, counts)

    source = jnp.stack([rows, cotangent])
    packed = jnp.sum(
        jnp.where(
            table[:, None, :, :, :, None], source[None, :, None].astype(F32), 0.0
        ),
        axis=4,
    ).astype(BF16)
    packed = packed.reshape(2, 1, 2 * per_owner, width)
    send = jnp.broadcast_to(packed, (2, size_z, 2 * per_owner, width))
    recv = lax.all_to_all(
        send.reshape(near, 2 * per_owner, width), NEAR, 0, 0, tiled=True
    )
    recv = recv.reshape(near, 2, per_owner, width).transpose(1, 0, 2, 3)
    every = lax.all_gather(recv.reshape(2, block, width), "hidden_x", axis=0, tiled=False)
    flat_rows = every[:, 0].reshape(slots, width)
    flat_cot = every[:, 1].reshape(slots, width)

    parts = jnp.stack(
        [
            contract(gate_weight, flat_rows, 0, 1),
            contract(up_weight, flat_rows, 0, 1),
            contract(down_weight, flat_cot, 1, 1),
        ]
    )
    parts = parts.reshape(3, size_y, size_c, share_units, slots).transpose(2, 1, 0, 3, 4)
    parts = with_layout_constraint(parts, Layout(major_to_minor=(0, 1, 2, 3, 4)))
    pair = lax.all_to_all(parts, "width_core", 0, 0, tiled=True)
    pair = pair[0] + pair[1]
    sent = lax.all_to_all(pair.astype(BF16), "width_y", 0, 0, tiled=True)
    gate, up_value, dhid = own_kept(pair, sent, "width_y")
    sigma = jax.nn.sigmoid(gate)
    silu = gate * sigma
    share = jnp.stack(
        [
            (silu * up_value).astype(BF16),
            (dhid * up_value * sigma * (1.0 + gate * (1.0 - sigma))).astype(BF16),
            (dhid * silu).astype(BF16),
        ]
    )
    acts = lax.all_gather(share, WIDTH, axis=0, tiled=False)
    hidden = acts[:, 0].reshape(units, slots)
    dgate = acts[:, 1].reshape(units, slots)
    dup = acts[:, 2].reshape(units, slots)

    place_x = lax.axis_index("hidden_x")
    sent, own = second_products(
        place_x.reshape(1), acts, gate_weight, up_weight, down_weight, size_x
    )
    sent = lax.all_to_all(
        sent.reshape(size_x, near, 8, width), "hidden_x", 0, 0, tiled=True
    )
    grad_gate = contract(flat_rows, dgate, 0, 1)
    grad_up = contract(flat_rows, dup, 0, 1)
    grad_down = contract(hidden, flat_cot, 1, 0)
    other = lax.broadcasted_iota(jnp.int32, (size_x, 1, 1, 1), 0) != place_x
    result = jnp.sum(jnp.where(other, sent.astype(F32), 0.0), axis=0)
    result = (own.reshape(near, 8, width) + result).astype(BF16)
    result = lax.all_to_all(result, NEAR, 0, 0, tiled=True)
    result = jnp.sum(
        result.reshape(2, size_z, 2, CAP, mb, width).astype(F32), axis=1
    )
    result = lax.optimization_barrier(result).astype(BF16)
    finals = []
    for which in (0, 1):
        per_row = []
        for p in range(row_dev):
            value = jnp.zeros((), BF16)
            for branch in (0, 1):
                for s in range(CAP):
                    value = jnp.where(
                        table[branch, s, :, p : p + 1], result[branch, which, s], value
                    )
            per_row.append(value)
        finals.append(jnp.stack(per_row, axis=1))
    return (finals[0], finals[1], grad_gate[None], grad_up[None], grad_down[None])


def solution(mesh):
    mesh = Mesh(mesh.devices.reshape((2,) + SUB), NAMES)
    owner_rows = P(None, OWNERS, WIDTH)
    return jax.shard_map(
        shards,
        mesh=mesh,
        in_specs=(
            owner_rows,
            owner_rows,
            P(None, OWNERS),
            P(None, OWNERS),
            P("branch", WIDTH, HIDDEN),
            P("branch", WIDTH, HIDDEN),
            P("branch", HIDDEN, WIDTH),
        ),
        out_specs=(
            owner_rows,
            owner_rows,
            P("branch", WIDTH, HIDDEN),
            P("branch", WIDTH, HIDDEN),
            P("branch", HIDDEN, WIDTH),
        ),
        check_vma=False,
    )
```

```python
import jax
import jax.numpy as jnp
from jax import lax
from jax.experimental import pallas as pl
from jax.experimental.layout import Layout, with_layout_constraint
from jax.experimental.pallas import tpu as pltpu
from jax.sharding import Mesh, PartitionSpec as P

CAP = 2
BF16 = jnp.bfloat16
F32 = jnp.float32
SUB = (4, 12, 4, 2)
NAMES = ("branch", "hidden_x", "hidden_z", "width_y", "width_core")
HIDDEN = ("hidden_x", "hidden_z")
WIDTH = ("width_y", "width_core")
OWNERS = ("branch",) + HIDDEN
NEAR = ("branch", "hidden_z")


def slot_table(labels, counts):
    mb, row_dev = labels.shape
    shape = (2, mb, row_dev, row_dev)
    branch, _, here, other = (lax.broadcasted_iota(jnp.int32, shape, d) for d in range(4))
    counted = (other < counts[None, :, :, None]) & (labels[None, :, None, :] == branch)
    rank = jnp.sum(jnp.where(counted & (other < here), 1, 0), axis=3)
    own = jnp.sum(jnp.where(counted & (other == here), 1, 0), axis=3)
    rank = jnp.where(own == 1, rank, -1)
    slot = lax.broadcasted_iota(jnp.int32, (2, CAP, mb, row_dev), 1)
    return rank[:, None] == slot


def contract(left, right, left_dim, right_dim):
    return lax.dot_general(
        left, right, (((left_dim,), (right_dim,)), ((), ())), preferred_element_type=F32
    )


def own_kept(own, received, axis):
    place = lax.broadcasted_iota(jnp.int32, own.shape, 0)
    mine = place == lax.axis_index(axis)
    return jnp.sum(jnp.where(mine, own, received.astype(F32)), axis=0)


def full(shape):
    return pl.BlockSpec(shape, lambda: (0,) * len(shape))


def second_kernel(place_ref, acts_ref, gate_ref, up_ref, down_ref, sent_ref, own_ref, scratch):
    parts, kinds, share_units, slots = acts_ref.shape
    units = parts * share_units
    width = down_ref.shape[1]
    hidden = acts_ref[:, 0].reshape(units, slots)
    dgate = acts_ref[:, 1].reshape(units, slots)
    dup = acts_ref[:, 2].reshape(units, slots)
    out = contract(hidden, down_ref[...], 0, 0)
    back = contract(dgate, gate_ref[...], 0, 1) + contract(dup, up_ref[...], 0, 1)
    tiles = slots // 8
    out = out.reshape(tiles, 8, width)
    back = back.reshape(tiles, 8, width)
    first = lax.broadcasted_iota(jnp.int32, out.shape, 1) < 4
    even = jnp.where(first, out, pltpu.roll(back, 4, 1))
    odd = jnp.where(first, pltpu.roll(out, 4, 1), back)
    sent_ref[:, 0] = even.astype(BF16)
    sent_ref[:, 1] = odd.astype(BF16)
    scratch[:, 0] = even
    scratch[:, 1] = odd
    own_tiles = own_ref.shape[0]
    own_ref[...] = scratch[pl.ds(place_ref[0] * own_tiles, own_tiles)]


def second_products(place, acts, gate_weight, up_weight, down_weight, size_x):
    slots = acts.shape[3]
    width = down_weight.shape[1]
    shape = (slots // 8, 2, 8, width)
    own_shape = (slots // 8 // size_x, 2, 8, width)
    return pl.pallas_call(
        second_kernel,
        out_shape=(
            jax.ShapeDtypeStruct(shape, BF16),
            jax.ShapeDtypeStruct(own_shape, F32),
        ),
        in_specs=[
            pl.BlockSpec(memory_space=pltpu.SMEM),
            full(acts.shape),
            full(gate_weight.shape),
            full(up_weight.shape),
            full(down_weight.shape),
        ],
        out_specs=(full(shape), full(own_shape)),
        scratch_shapes=[pltpu.VMEM(shape, F32)],
        compiler_params=pltpu.CompilerParams(vmem_limit_bytes=12 * 1024 * 1024),
        name="second_products",
    )(place, acts, gate_weight, up_weight, down_weight)


def shards(rows, cotangent, labels, counts, gate_weight, up_weight, down_weight):
    gate_weight, up_weight, down_weight = gate_weight[0], up_weight[0], down_weight[0]
    mb, row_dev, width = rows.shape
    size_x, size_z = lax.axis_size("hidden_x"), lax.axis_size("hidden_z")
    size_y, size_c = lax.axis_size("width_y"), lax.axis_size("width_core")
    near = 2 * size_z
    per_owner = mb * CAP
    block = near * per_owner
    slots = size_x * block
    units = gate_weight.shape[1]
    share_units = units // (size_y * size_c)
    table = slot_table(labels, counts)

    source = jnp.stack([rows, cotangent])
    packed = jnp.sum(
        jnp.where(
            table[:, None, :, :, :, None], source[None, :, None].astype(F32), 0.0
        ),
        axis=4,
    ).astype(BF16)
    packed = packed.reshape(2, 1, 2 * per_owner, width)
    send = jnp.broadcast_to(packed, (2, size_z, 2 * per_owner, width))
    recv = lax.all_to_all(
        send.reshape(near, 2 * per_owner, width), NEAR, 0, 0, tiled=True
    )
    recv = recv.reshape(near, 2, per_owner, width).transpose(1, 0, 2, 3)
    every = lax.all_gather(recv.reshape(2, block, width), "hidden_x", axis=0, tiled=False)
    flat_rows = every[:, 0].reshape(slots, width)
    flat_cot = every[:, 1].reshape(slots, width)

    parts = jnp.stack(
        [
            contract(gate_weight, flat_rows, 0, 1),
            contract(up_weight, flat_rows, 0, 1),
            contract(down_weight, flat_cot, 1, 1),
        ]
    )
    parts = parts.reshape(3, size_y, size_c, share_units, slots).transpose(2, 1, 0, 3, 4)
    parts = with_layout_constraint(parts, Layout(major_to_minor=(0, 1, 2, 3, 4)))
    pair = lax.all_to_all(parts, "width_core", 0, 0, tiled=True)
    pair = pair[0] + pair[1]
    sent = lax.all_to_all(pair.astype(BF16), "width_y", 0, 0, tiled=True)
    gate, up_value, dhid = own_kept(pair, sent, "width_y")
    sigma = jax.nn.sigmoid(gate)
    silu = gate * sigma
    share = jnp.stack(
        [
            (silu * up_value).astype(BF16),
            (dhid * up_value * sigma * (1.0 + gate * (1.0 - sigma))).astype(BF16),
            (dhid * silu).astype(BF16),
        ]
    )
    acts = lax.all_gather(share, WIDTH, axis=0, tiled=False)
    hidden = acts[:, 0].reshape(units, slots)
    dgate = acts[:, 1].reshape(units, slots)
    dup = acts[:, 2].reshape(units, slots)

    place_x = lax.axis_index("hidden_x")
    sent, own = second_products(
        place_x.reshape(1), acts, gate_weight, up_weight, down_weight, size_x
    )
    sent = lax.all_to_all(
        sent.reshape(size_x, near, 8, width), "hidden_x", 0, 0, tiled=True
    )
    grad_gate = contract(flat_rows, dgate, 0, 1)
    grad_up = contract(flat_rows, dup, 0, 1)
    grad_down = contract(hidden, flat_cot, 1, 0)
    other = lax.broadcasted_iota(jnp.int32, (size_x, 1, 1, 1), 0) != place_x
    result = jnp.sum(jnp.where(other, sent.astype(F32), 0.0), axis=0)
    result = (own.reshape(near, 8, width) + result).astype(BF16)
    result = lax.all_to_all(result, NEAR, 0, 0, tiled=True)
    result = jnp.sum(
        result.reshape(2, size_z, 2, CAP, mb, width).astype(F32), axis=1
    )
    result = lax.optimization_barrier(result).astype(BF16)
    finals = []
    for which in (0, 1):
        per_row = []
        for p in range(row_dev):
            value = jnp.zeros((), BF16)
            for branch in (0, 1):
                for s in range(CAP):
                    value = jnp.where(
                        table[branch, s, :, p : p + 1], result[branch, which, s], value
                    )
            per_row.append(value)
        finals.append(jnp.stack(per_row, axis=1))
    return (finals[0], finals[1], grad_gate[None], grad_up[None], grad_down[None])


def solution(mesh):
    mesh = Mesh(mesh.devices.reshape((2,) + SUB), NAMES)
    owner_rows = P(None, OWNERS, WIDTH)
    return jax.shard_map(
        shards,
        mesh=mesh,
        in_specs=(
            owner_rows,
            owner_rows,
            P(None, OWNERS),
            P(None, OWNERS),
            P("branch", WIDTH, HIDDEN),
            P("branch", WIDTH, HIDDEN),
            P("branch", HIDDEN, WIDTH),
        ),
        out_specs=(
            owner_rows,
            owner_rows,
            P("branch", WIDTH, HIDDEN),
            P("branch", WIDTH, HIDDEN),
            P("branch", HIDDEN, WIDTH),
        ),
        check_vma=False,
    )
```

```python
import jax
import jax.numpy as jnp
from jax import lax
from jax.experimental import pallas as pl
from jax.experimental.layout import Layout, with_layout_constraint
from jax.experimental.pallas import tpu as pltpu
from jax.sharding import Mesh, PartitionSpec as P

CAP = 2
BF16 = jnp.bfloat16
F32 = jnp.float32
SUB = (4, 12, 4, 2)
NAMES = ("branch", "hidden_x", "hidden_z", "width_y", "width_core")
HIDDEN = ("hidden_x", "hidden_z")
WIDTH = ("width_y", "width_core")
OWNERS = ("branch",) + HIDDEN
NEAR = ("branch", "hidden_z")


def slot_table(labels, counts):
    mb, row_dev = labels.shape
    shape = (2, mb, row_dev, row_dev)
    branch, _, here, other = (lax.broadcasted_iota(jnp.int32, shape, d) for d in range(4))
    counted = (other < counts[None, :, :, None]) & (labels[None, :, None, :] == branch)
    rank = jnp.sum(jnp.where(counted & (other < here), 1, 0), axis=3)
    own = jnp.sum(jnp.where(counted & (other == here), 1, 0), axis=3)
    rank = jnp.where(own == 1, rank, -1)
    slot = lax.broadcasted_iota(jnp.int32, (2, CAP, mb, row_dev), 1)
    return rank[:, None] == slot


def contract(left, right, left_dim, right_dim):
    return lax.dot_general(
        left, right, (((left_dim,), (right_dim,)), ((), ())), preferred_element_type=F32
    )


def full(shape):
    return pl.BlockSpec(shape, lambda: (0,) * len(shape))


def second_kernel(place_ref, acts_ref, gate_ref, up_ref, down_ref, sent_ref, own_ref, scratch):
    parts, kinds, share_units, slots = acts_ref.shape
    units = parts * share_units
    width = down_ref.shape[1]
    hidden = acts_ref[:, 0].reshape(units, slots)
    dgate = acts_ref[:, 1].reshape(units, slots)
    dup = acts_ref[:, 2].reshape(units, slots)
    out = contract(hidden, down_ref[...], 0, 0)
    back = contract(dgate, gate_ref[...], 0, 1) + contract(dup, up_ref[...], 0, 1)
    tiles = slots // 8
    out = out.reshape(tiles, 8, width)
    back = back.reshape(tiles, 8, width)
    first = lax.broadcasted_iota(jnp.int32, out.shape, 1) < 4
    even = jnp.where(first, out, pltpu.roll(back, 4, 1))
    odd = jnp.where(first, pltpu.roll(out, 4, 1), back)
    sent_ref[:, 0] = even.astype(BF16)
    sent_ref[:, 1] = odd.astype(BF16)
    scratch[:, 0] = even
    scratch[:, 1] = odd
    own_tiles = own_ref.shape[0]
    own_ref[...] = scratch[pl.ds(place_ref[0] * own_tiles, own_tiles)]


def second_products(place, acts, gate_weight, up_weight, down_weight, size_x):
    slots = acts.shape[3]
    width = down_weight.shape[1]
    shape = (slots // 8, 2, 8, width)
    own_shape = (slots // 8 // size_x, 2, 8, width)
    return pl.pallas_call(
        second_kernel,
        out_shape=(
            jax.ShapeDtypeStruct(shape, BF16),
            jax.ShapeDtypeStruct(own_shape, F32),
        ),
        in_specs=[
            pl.BlockSpec(memory_space=pltpu.SMEM),
            full(acts.shape),
            full(gate_weight.shape),
            full(up_weight.shape),
            full(down_weight.shape),
        ],
        out_specs=(full(shape), full(own_shape)),
        scratch_shapes=[pltpu.VMEM(shape, F32)],
        compiler_params=pltpu.CompilerParams(vmem_limit_bytes=12 * 1024 * 1024),
        name="second_products",
    )(place, acts, gate_weight, up_weight, down_weight)


def shards(rows, cotangent, labels, counts, gate_weight, up_weight, down_weight):
    gate_weight, up_weight, down_weight = gate_weight[0], up_weight[0], down_weight[0]
    mb, row_dev, width = rows.shape
    size_x, size_z = lax.axis_size("hidden_x"), lax.axis_size("hidden_z")
    size_y, size_c = lax.axis_size("width_y"), lax.axis_size("width_core")
    near = 2 * size_z
    per_owner = mb * CAP
    block = near * per_owner
    slots = size_x * block
    units = gate_weight.shape[1]
    table = slot_table(labels, counts)

    source = jnp.stack([rows, cotangent])
    packed = jnp.sum(
        jnp.where(
            table[:, None, :, :, :, None], source[None, :, None].astype(F32), 0.0
        ),
        axis=4,
    ).astype(BF16)
    packed = packed.reshape(2, 1, 2 * per_owner, width)
    send = jnp.broadcast_to(packed, (2, size_z, 2 * per_owner, width))
    recv = lax.all_to_all(
        send.reshape(near, 2 * per_owner, width), NEAR, 0, 0, tiled=True
    )
    recv = recv.reshape(near, 2, per_owner, width).transpose(1, 0, 2, 3)
    every = lax.all_gather(recv.reshape(2, block, width), "hidden_x", axis=0, tiled=False)
    flat_rows = every[:, 0].reshape(slots, width)
    flat_cot = every[:, 1].reshape(slots, width)

    parts = jnp.stack(
        [
            contract(gate_weight, flat_rows, 0, 1),
            contract(up_weight, flat_rows, 0, 1),
            contract(down_weight, flat_cot, 1, 1),
        ]
    )
    half = units // size_c
    parts = parts.reshape(3, size_c, half, slots).transpose(1, 0, 2, 3)
    parts = with_layout_constraint(parts, Layout(major_to_minor=(0, 1, 2, 3)))
    pair = lax.all_to_all(parts, "width_core", 0, 0, tiled=True)
    pair = pair[0] + pair[1]
    sent = jnp.broadcast_to(pair.astype(BF16), (size_y,) + pair.shape)
    sent = lax.all_to_all(sent, "width_y", 0, 0, tiled=True)
    place_y = lax.axis_index("width_y")
    other = lax.broadcasted_iota(jnp.int32, (size_y, 1, 1, 1), 0) != place_y
    gate, up_value, dhid = pair + jnp.sum(
        jnp.where(other, sent.astype(F32), 0.0), axis=0
    )
    sigma = jax.nn.sigmoid(gate)
    silu = gate * sigma
    share = jnp.stack(
        [
            (silu * up_value).astype(BF16),
            (dhid * up_value * sigma * (1.0 + gate * (1.0 - sigma))).astype(BF16),
            (dhid * silu).astype(BF16),
        ]
    )
    acts = lax.all_gather(share, "width_core", axis=0, tiled=False)
    hidden = acts[:, 0].reshape(units, slots)
    dgate = acts[:, 1].reshape(units, slots)
    dup = acts[:, 2].reshape(units, slots)

    place_x = lax.axis_index("hidden_x")
    sent, own = second_products(
        place_x.reshape(1), acts, gate_weight, up_weight, down_weight, size_x
    )
    sent = lax.all_to_all(
        sent.reshape(size_x, near, 8, width), "hidden_x", 0, 0, tiled=True
    )
    grad_gate = contract(flat_rows, dgate, 0, 1)
    grad_up = contract(flat_rows, dup, 0, 1)
    grad_down = contract(hidden, flat_cot, 1, 0)
    other = lax.broadcasted_iota(jnp.int32, (size_x, 1, 1, 1), 0) != place_x
    result = jnp.sum(jnp.where(other, sent.astype(F32), 0.0), axis=0)
    result = (own.reshape(near, 8, width) + result).astype(BF16)
    result = lax.all_to_all(result, NEAR, 0, 0, tiled=True)
    result = jnp.sum(
        result.reshape(2, size_z, 2, CAP, mb, width).astype(F32), axis=1
    )
    result = lax.optimization_barrier(result).astype(BF16)
    finals = []
    for which in (0, 1):
        per_row = []
        for p in range(row_dev):
            value = jnp.zeros((), BF16)
            for branch in (0, 1):
                for s in range(CAP):
                    value = jnp.where(
                        table[branch, s, :, p : p + 1], result[branch, which, s], value
                    )
            per_row.append(value)
        finals.append(jnp.stack(per_row, axis=1))
    return (finals[0], finals[1], grad_gate[None], grad_up[None], grad_down[None])


def solution(mesh):
    mesh = Mesh(mesh.devices.reshape((2,) + SUB), NAMES)
    owner_rows = P(None, OWNERS, WIDTH)
    return jax.shard_map(
        shards,
        mesh=mesh,
        in_specs=(
            owner_rows,
            owner_rows,
            P(None, OWNERS),
            P(None, OWNERS),
            P("branch", WIDTH, HIDDEN),
            P("branch", WIDTH, HIDDEN),
            P("branch", HIDDEN, WIDTH),
        ),
        out_specs=(
            owner_rows,
            owner_rows,
            P("branch", WIDTH, HIDDEN),
            P("branch", WIDTH, HIDDEN),
            P("branch", HIDDEN, WIDTH),
        ),
        check_vma=False,
    )
```

```python
import jax
import jax.numpy as jnp
from jax import lax
from jax.experimental import pallas as pl
from jax.experimental.pallas import tpu as pltpu
from jax.sharding import Mesh, PartitionSpec as P

CAP = 2
BF16 = jnp.bfloat16
F32 = jnp.float32
SUB = (4, 12, 4, 2)
NAMES = ("branch", "hidden_x", "hidden_z", "width_y", "width_core")
HIDDEN = ("hidden_x", "hidden_z")
WIDTH = ("width_y", "width_core")
OWNERS = ("branch",) + HIDDEN
NEAR = ("branch", "hidden_z")


def slot_picks(labels_ref, counts_ref, shape):
    row_dev = labels_ref.shape[1]
    lower = lax.broadcasted_iota(jnp.int32, shape, 0) == 0
    picks = [[[None] * row_dev for _ in range(CAP)] for _ in range(2)]
    for branch in range(2):
        slot = []
        for m in range(2):
            seen = jnp.int32(0)
            places = []
            for p in range(row_dev):
                chosen = (p < counts_ref[0, m]) & (labels_ref[m, p] == branch)
                places.append(jnp.where(chosen, seen, -1))
                seen = seen + jnp.where(chosen, 1, 0)
            slot.append(places)
        for p in range(row_dev):
            place = jnp.where(lower, slot[0][p], slot[1][p])
            for s in range(CAP):
                picks[branch][s][p] = place == s
    return picks


def pack_kernel(
    labels_in, counts_in, rows_in, cot_in, send_ref,
    labels_ref, counts_ref, rows_ref, cot_ref, scratch, sems,
):
    row_dev, mb, width = rows_ref.shape
    copies = [
        pltpu.make_async_copy(source, target, sems.at[i])
        for i, (source, target) in enumerate(
            (
                (labels_in, labels_ref),
                (counts_in, counts_ref),
                (rows_in, rows_ref),
                (cot_in, cot_ref),
            )
        )
    ]
    for copy in copies:
        copy.start()
    for copy in copies:
        copy.wait()
    picks = slot_picks(labels_ref, counts_ref, (mb, width))
    sources = [
        [ref[p].astype(F32) for p in range(row_dev)] for ref in (rows_ref, cot_ref)
    ]
    for branch in range(2):
        for which in range(2):
            for s in range(CAP):
                value = jnp.zeros((mb, width), F32)
                for p in range(row_dev):
                    value = jnp.where(picks[branch][s][p], sources[which][p], value)
                scratch[branch, pl.ds((which * CAP + s) * mb, mb), :] = value
        tile = scratch[branch].astype(BF16)
        for peer in range(send_ref.shape[1]):
            send_ref[branch, peer] = tile


def finish_kernel(labels_ref, counts_ref, recv_ref, out_ref, back_ref, scratch):
    row_dev, mb, width = out_ref.shape
    peers = recv_ref.shape[0] // 2
    picks = slot_picks(labels_ref, counts_ref, (mb, width))
    for branch in range(2):
        total = recv_ref[branch * peers].astype(F32)
        for peer in range(1, peers):
            total = total + recv_ref[branch * peers + peer].astype(F32)
        scratch[branch] = total
    for which, ref in enumerate((out_ref, back_ref)):
        for p in range(row_dev):
            value = jnp.zeros((mb, width), F32)
            for branch in range(2):
                for s in range(CAP):
                    value = jnp.where(
                        picks[branch][s][p],
                        scratch[branch, pl.ds((which * CAP + s) * mb, mb), :],
                        value,
                    )
            ref[p] = value.astype(BF16)


def first_kernel(every_ref, gate_ref, up_ref, down_ref, parts_ref):
    size_x, _, block, width = every_ref.shape
    size_c, size_y, _, share_units, slots = parts_ref.shape
    rows = every_ref[:, 0].reshape(slots, width)
    cot = every_ref[:, 1].reshape(slots, width)
    sums = (
        contract(gate_ref[...], rows, 0, 1),
        contract(up_ref[...], rows, 0, 1),
        contract(down_ref[...], cot, 1, 1),
    )
    for kind, total in enumerate(sums):
        for y in range(size_y):
            for c in range(size_c):
                start = (y * size_c + c) * share_units
                parts_ref[c, y, kind] = total[start : start + share_units]


def contract(left, right, left_dim, right_dim):
    return lax.dot_general(
        left, right, (((left_dim,), (right_dim,)), ((), ())), preferred_element_type=F32
    )


def own_kept(own, received, axis):
    place = lax.broadcasted_iota(jnp.int32, own.shape, 0)
    mine = place == lax.axis_index(axis)
    return jnp.sum(jnp.where(mine, own, received.astype(F32)), axis=0)


def full(shape):
    return pl.BlockSpec(shape, lambda: (0,) * len(shape))


def second_kernel(place_ref, acts_ref, gate_ref, up_ref, down_ref, sent_ref, own_ref, scratch):
    parts, kinds, share_units, slots = acts_ref.shape
    units = parts * share_units
    width = down_ref.shape[1]
    hidden = acts_ref[:, 0].reshape(units, slots)
    dgate = acts_ref[:, 1].reshape(units, slots)
    dup = acts_ref[:, 2].reshape(units, slots)
    out = contract(hidden, down_ref[...], 0, 0)
    back = contract(dgate, gate_ref[...], 0, 1) + contract(dup, up_ref[...], 0, 1)
    tiles = slots // 8
    out = out.reshape(tiles, 8, width)
    back = back.reshape(tiles, 8, width)
    first = lax.broadcasted_iota(jnp.int32, out.shape, 1) < 4
    even = jnp.where(first, out, pltpu.roll(back, 4, 1))
    odd = jnp.where(first, pltpu.roll(out, 4, 1), back)
    sent_ref[:, 0] = even.astype(BF16)
    sent_ref[:, 1] = odd.astype(BF16)
    scratch[:, 0] = even
    scratch[:, 1] = odd
    own_tiles = own_ref.shape[0]
    own_ref[...] = scratch[pl.ds(place_ref[0] * own_tiles, own_tiles)]


GRANT = pltpu.CompilerParams(vmem_limit_bytes=12 * 1024 * 1024)
SCALARS = pl.BlockSpec(memory_space=pltpu.SMEM)


def pack(labels, counts, rows, cotangent, peers):
    row_dev, mb, width = rows.shape
    shape = (2, peers, 2 * CAP * mb, width)
    return pl.pallas_call(
        pack_kernel,
        out_shape=jax.ShapeDtypeStruct(shape, BF16),
        in_specs=[pl.BlockSpec(memory_space=pltpu.HBM)] * 4,
        out_specs=full(shape),
        scratch_shapes=[
            pltpu.SMEM(labels.shape, jnp.int32),
            pltpu.SMEM(counts.shape, jnp.int32),
            pltpu.VMEM(rows.shape, BF16),
            pltpu.VMEM(rows.shape, BF16),
            pltpu.VMEM((2, 2 * CAP * mb, width), F32),
            pltpu.SemaphoreType.DMA((4,)),
        ],
        name="pack",
    )(labels, counts, rows, cotangent)


def finish(labels, counts, recv, mb):
    shape = (labels.shape[1], mb, recv.shape[2])
    return pl.pallas_call(
        finish_kernel,
        out_shape=(jax.ShapeDtypeStruct(shape, BF16),) * 2,
        in_specs=[SCALARS, SCALARS, full(recv.shape)],
        out_specs=(full(shape),) * 2,
        scratch_shapes=[pltpu.VMEM((2,) + recv.shape[1:], F32)],
        compiler_params=GRANT,
        name="finish",
    )(labels, counts, recv)


def first_products(every, gate_weight, up_weight, down_weight, size_c, size_y):
    units = gate_weight.shape[1]
    slots = every.shape[0] * every.shape[2]
    shape = (size_c, size_y, 3, units // (size_c * size_y), slots)
    return pl.pallas_call(
        first_kernel,
        out_shape=jax.ShapeDtypeStruct(shape, F32),
        in_specs=[
            full(every.shape),
            full(gate_weight.shape),
            full(up_weight.shape),
            full(down_weight.shape),
        ],
        out_specs=full(shape),
        compiler_params=GRANT,
        name="first_products",
    )(every, gate_weight, up_weight, down_weight)


def second_products(place, acts, gate_weight, up_weight, down_weight, size_x):
    slots = acts.shape[3]
    width = down_weight.shape[1]
    shape = (slots // 8, 2, 8, width)
    own_shape = (slots // 8 // size_x, 2, 8, width)
    return pl.pallas_call(
        second_kernel,
        out_shape=(
            jax.ShapeDtypeStruct(shape, BF16),
            jax.ShapeDtypeStruct(own_shape, F32),
        ),
        in_specs=[
            pl.BlockSpec(memory_space=pltpu.SMEM),
            full(acts.shape),
            full(gate_weight.shape),
            full(up_weight.shape),
            full(down_weight.shape),
        ],
        out_specs=(full(shape), full(own_shape)),
        scratch_shapes=[pltpu.VMEM(shape, F32)],
        compiler_params=GRANT,
        name="second_products",
    )(place, acts, gate_weight, up_weight, down_weight)


def shards(rows, cotangent, labels, counts, gate_weight, up_weight, down_weight):
    gate_weight, up_weight, down_weight = gate_weight[0], up_weight[0], down_weight[0]
    mb, _, width = rows.shape
    size_x, size_z = lax.axis_size("hidden_x"), lax.axis_size("hidden_z")
    size_y, size_c = lax.axis_size("width_y"), lax.axis_size("width_core")
    near = 2 * size_z
    counts = counts.T
    per_owner = mb * CAP
    block = near * per_owner
    slots = size_x * block
    units = gate_weight.shape[1]

    send = pack(
        labels, counts, rows.transpose(1, 0, 2), cotangent.transpose(1, 0, 2), size_z
    )
    recv = lax.all_to_all(
        send.reshape(near, 2 * per_owner, width), NEAR, 0, 0, tiled=True
    )
    recv = recv.reshape(near, 2, per_owner, width).transpose(1, 0, 2, 3)
    every = lax.all_gather(recv.reshape(2, block, width), "hidden_x", axis=0, tiled=False)
    flat_rows = every[:, 0].reshape(slots, width)
    flat_cot = every[:, 1].reshape(slots, width)

    parts = first_products(every, gate_weight, up_weight, down_weight, size_c, size_y)
    pair = lax.all_to_all(parts, "width_core", 0, 0, tiled=True)
    pair = pair[0] + pair[1]
    sent = lax.all_to_all(pair.astype(BF16), "width_y", 0, 0, tiled=True)
    gate, up_value, dhid = own_kept(pair, sent, "width_y")
    sigma = jax.nn.sigmoid(gate)
    silu = gate * sigma
    share = jnp.stack(
        [
            (silu * up_value).astype(BF16),
            (dhid * up_value * sigma * (1.0 + gate * (1.0 - sigma))).astype(BF16),
            (dhid * silu).astype(BF16),
        ]
    )
    acts = lax.all_gather(share, WIDTH, axis=0, tiled=False)
    hidden = acts[:, 0].reshape(units, slots)
    dgate = acts[:, 1].reshape(units, slots)
    dup = acts[:, 2].reshape(units, slots)

    place_x = lax.axis_index("hidden_x")
    sent, own = second_products(
        place_x.reshape(1), acts, gate_weight, up_weight, down_weight, size_x
    )
    sent = lax.all_to_all(
        sent.reshape(size_x, near, 8, width), "hidden_x", 0, 0, tiled=True
    )
    grad_gate = contract(flat_rows, dgate, 0, 1)
    grad_up = contract(flat_rows, dup, 0, 1)
    grad_down = contract(hidden, flat_cot, 1, 0)
    other = lax.broadcasted_iota(jnp.int32, (size_x, 1, 1, 1), 0) != place_x
    result = jnp.sum(jnp.where(other, sent.astype(F32), 0.0), axis=0)
    result = (own.reshape(near, 8, width) + result).astype(BF16)
    result = lax.all_to_all(result, NEAR, 0, 0, tiled=True)
    output, grad_rows = finish(labels, counts, result, mb)
    return (
        output.transpose(1, 0, 2),
        grad_rows.transpose(1, 0, 2),
        grad_gate[None],
        grad_up[None],
        grad_down[None],
    )


def solution(mesh):
    mesh = Mesh(mesh.devices.reshape((2,) + SUB), NAMES)
    owner_rows = P(None, OWNERS, WIDTH)
    return jax.shard_map(
        shards,
        mesh=mesh,
        in_specs=(
            owner_rows,
            owner_rows,
            P(None, OWNERS),
            P(None, OWNERS),
            P("branch", WIDTH, HIDDEN),
            P("branch", WIDTH, HIDDEN),
            P("branch", HIDDEN, WIDTH),
        ),
        out_specs=(
            owner_rows,
            owner_rows,
            P("branch", WIDTH, HIDDEN),
            P("branch", WIDTH, HIDDEN),
            P("branch", HIDDEN, WIDTH),
        ),
        check_vma=False,
    )
```

```python
import jax
import jax.numpy as jnp
from jax import lax
from jax.experimental import pallas as pl
from jax.experimental.pallas import tpu as pltpu
from jax.sharding import Mesh, PartitionSpec as P

CAP = 2
BF16 = jnp.bfloat16
F32 = jnp.float32
SUB = (4, 12, 4, 2)
NAMES = ("branch", "hidden_x", "hidden_z", "width_y", "width_core")
HIDDEN = ("hidden_x", "hidden_z")
WIDTH = ("width_y", "width_core")
OWNERS = ("branch",) + HIDDEN
NEAR = ("branch", "hidden_z")


def slot_picks(labels_ref, counts_ref, shape):
    row_dev = labels_ref.shape[1]
    lower = lax.broadcasted_iota(jnp.int32, shape, 0) == 0
    picks = [[[None] * row_dev for _ in range(CAP)] for _ in range(2)]
    for branch in range(2):
        slot = []
        for m in range(2):
            seen = jnp.int32(0)
            places = []
            for p in range(row_dev):
                chosen = (p < counts_ref[0, m]) & (labels_ref[m, p] == branch)
                places.append(jnp.where(chosen, seen, -1))
                seen = seen + jnp.where(chosen, 1, 0)
            slot.append(places)
        for p in range(row_dev):
            place = jnp.where(lower, slot[0][p], slot[1][p])
            for s in range(CAP):
                picks[branch][s][p] = place == s
    return picks


def pack_kernel(
    labels_in, counts_in, rows_in, cot_in, send_ref,
    labels_ref, counts_ref, rows_ref, cot_ref, scratch, sems,
):
    row_dev, mb, width = rows_ref.shape
    copies = [
        pltpu.make_async_copy(source, target, sems.at[i])
        for i, (source, target) in enumerate(
            (
                (labels_in, labels_ref),
                (counts_in, counts_ref),
                (rows_in, rows_ref),
                (cot_in, cot_ref),
            )
        )
    ]
    for copy in copies:
        copy.start()
    for copy in copies:
        copy.wait()
    picks = slot_picks(labels_ref, counts_ref, (mb, width))
    sources = [
        [ref[p].astype(F32) for p in range(row_dev)] for ref in (rows_ref, cot_ref)
    ]
    for branch in range(2):
        for which in range(2):
            for s in range(CAP):
                value = jnp.zeros((mb, width), F32)
                for p in range(row_dev):
                    value = jnp.where(picks[branch][s][p], sources[which][p], value)
                scratch[branch, pl.ds((which * CAP + s) * mb, mb), :] = value
        tile = scratch[branch].astype(BF16)
        for peer in range(send_ref.shape[1]):
            send_ref[branch, peer] = tile


def finish_kernel(labels_ref, counts_ref, recv_ref, out_ref, back_ref, scratch):
    row_dev, mb, width = out_ref.shape
    peers = recv_ref.shape[0] // 2
    picks = slot_picks(labels_ref, counts_ref, (mb, width))
    for branch in range(2):
        total = recv_ref[branch * peers].astype(F32)
        for peer in range(1, peers):
            total = total + recv_ref[branch * peers + peer].astype(F32)
        scratch[branch] = total
    for which, ref in enumerate((out_ref, back_ref)):
        for p in range(row_dev):
            value = jnp.zeros((mb, width), F32)
            for branch in range(2):
                for s in range(CAP):
                    value = jnp.where(
                        picks[branch][s][p],
                        scratch[branch, pl.ds((which * CAP + s) * mb, mb), :],
                        value,
                    )
            ref[p] = value.astype(BF16)


def first_kernel(every_ref, gate_ref, up_ref, down_ref, parts_ref):
    size_x, _, block, width = every_ref.shape
    size_c, pieces, _, piece_units, slots = parts_ref.shape
    rows = every_ref[:, 0].reshape(slots, width)
    cot = every_ref[:, 1].reshape(slots, width)
    sums = (
        contract(gate_ref[...], rows, 0, 1),
        contract(up_ref[...], rows, 0, 1),
        contract(down_ref[...], cot, 1, 1),
    )
    for kind, total in enumerate(sums):
        for c in range(size_c):
            for piece in range(pieces):
                start = (c * pieces + piece) * piece_units
                parts_ref[c, piece, kind] = total[start : start + piece_units]


def contract(left, right, left_dim, right_dim):
    return lax.dot_general(
        left, right, (((left_dim,), (right_dim,)), ((), ())), preferred_element_type=F32
    )


def full(shape):
    return pl.BlockSpec(shape, lambda: (0,) * len(shape))


def second_kernel(place_ref, acts_ref, gate_ref, up_ref, down_ref, sent_ref, own_ref, scratch):
    size_c, pieces, _, piece_units, slots = acts_ref.shape
    units = size_c * pieces * piece_units
    width = down_ref.shape[1]
    hidden = acts_ref[:, :, 0].reshape(units, slots)
    dgate = acts_ref[:, :, 1].reshape(units, slots)
    dup = acts_ref[:, :, 2].reshape(units, slots)
    out = contract(hidden, down_ref[...], 0, 0)
    back = contract(dgate, gate_ref[...], 0, 1) + contract(dup, up_ref[...], 0, 1)
    tiles = slots // 8
    out = out.reshape(tiles, 8, width)
    back = back.reshape(tiles, 8, width)
    first = lax.broadcasted_iota(jnp.int32, out.shape, 1) < 4
    even = jnp.where(first, out, pltpu.roll(back, 4, 1))
    odd = jnp.where(first, pltpu.roll(out, 4, 1), back)
    sent_ref[:, 0] = even.astype(BF16)
    sent_ref[:, 1] = odd.astype(BF16)
    scratch[:, 0] = even
    scratch[:, 1] = odd
    own_tiles = own_ref.shape[0]
    own_ref[...] = scratch[pl.ds(place_ref[0] * own_tiles, own_tiles)]


GRANT = pltpu.CompilerParams(vmem_limit_bytes=12 * 1024 * 1024)
SCALARS = pl.BlockSpec(memory_space=pltpu.SMEM)


def pack(labels, counts, rows, cotangent, peers):
    row_dev, mb, width = rows.shape
    shape = (2, peers, 2 * CAP * mb, width)
    return pl.pallas_call(
        pack_kernel,
        out_shape=jax.ShapeDtypeStruct(shape, BF16),
        in_specs=[pl.BlockSpec(memory_space=pltpu.HBM)] * 4,
        out_specs=full(shape),
        scratch_shapes=[
            pltpu.SMEM(labels.shape, jnp.int32),
            pltpu.SMEM(counts.shape, jnp.int32),
            pltpu.VMEM(rows.shape, BF16),
            pltpu.VMEM(rows.shape, BF16),
            pltpu.VMEM((2, 2 * CAP * mb, width), F32),
            pltpu.SemaphoreType.DMA((4,)),
        ],
        name="pack",
    )(labels, counts, rows, cotangent)


def finish(labels, counts, recv, mb):
    shape = (labels.shape[1], mb, recv.shape[2])
    return pl.pallas_call(
        finish_kernel,
        out_shape=(jax.ShapeDtypeStruct(shape, BF16),) * 2,
        in_specs=[SCALARS, SCALARS, full(recv.shape)],
        out_specs=(full(shape),) * 2,
        scratch_shapes=[pltpu.VMEM((2,) + recv.shape[1:], F32)],
        compiler_params=GRANT,
        name="finish",
    )(labels, counts, recv)


def first_products(every, gate_weight, up_weight, down_weight, size_c):
    units = gate_weight.shape[1]
    slots = every.shape[0] * every.shape[2]
    shape = (size_c, 2, 3, units // (2 * size_c), slots)
    return pl.pallas_call(
        first_kernel,
        out_shape=jax.ShapeDtypeStruct(shape, F32),
        in_specs=[
            full(every.shape),
            full(gate_weight.shape),
            full(up_weight.shape),
            full(down_weight.shape),
        ],
        out_specs=full(shape),
        compiler_params=GRANT,
        name="first_products",
    )(every, gate_weight, up_weight, down_weight)


def second_products(place, acts, gate_weight, up_weight, down_weight, size_x):
    slots = acts.shape[4]
    width = down_weight.shape[1]
    shape = (slots // 8, 2, 8, width)
    own_shape = (slots // 8 // size_x, 2, 8, width)
    return pl.pallas_call(
        second_kernel,
        out_shape=(
            jax.ShapeDtypeStruct(shape, BF16),
            jax.ShapeDtypeStruct(own_shape, F32),
        ),
        in_specs=[
            pl.BlockSpec(memory_space=pltpu.SMEM),
            full(acts.shape),
            full(gate_weight.shape),
            full(up_weight.shape),
            full(down_weight.shape),
        ],
        out_specs=(full(shape), full(own_shape)),
        scratch_shapes=[pltpu.VMEM(shape, F32)],
        compiler_params=GRANT,
        name="second_products",
    )(place, acts, gate_weight, up_weight, down_weight)


def shards(rows, cotangent, labels, counts, gate_weight, up_weight, down_weight):
    gate_weight, up_weight, down_weight = gate_weight[0], up_weight[0], down_weight[0]
    mb, _, width = rows.shape
    size_x, size_z = lax.axis_size("hidden_x"), lax.axis_size("hidden_z")
    size_y, size_c = lax.axis_size("width_y"), lax.axis_size("width_core")
    near = 2 * size_z
    counts = counts.T
    per_owner = mb * CAP
    block = near * per_owner
    slots = size_x * block
    units = gate_weight.shape[1]

    send = pack(
        labels, counts, rows.transpose(1, 0, 2), cotangent.transpose(1, 0, 2), size_z
    )
    recv = lax.all_to_all(
        send.reshape(near, 2 * per_owner, width), NEAR, 0, 0, tiled=True
    )
    recv = recv.reshape(near, 2, per_owner, width).transpose(1, 0, 2, 3)
    every = lax.all_gather(recv.reshape(2, block, width), "hidden_x", axis=0, tiled=False)
    flat_rows = every[:, 0].reshape(slots, width)
    flat_cot = every[:, 1].reshape(slots, width)

    parts = first_products(every, gate_weight, up_weight, down_weight, size_c)
    pair = lax.all_to_all(parts, "width_core", 0, 0, tiled=True)
    pair = pair[0] + pair[1]
    low = [(i, i ^ 1) for i in range(size_y)]
    high = [(i, (i + 1 if i % 2 else i - 1) % size_y) for i in range(size_y)]
    sums = [pair[0], pair[1]]
    for routes in ((low, high), (high, low)):
        sums = [
            own + lax.ppermute(own.astype(BF16), "width_y", route).astype(F32)
            for own, route in zip(sums, routes)
        ]
    share = []
    for gate, up_value, dhid in sums:
        sigma = jax.nn.sigmoid(gate)
        silu = gate * sigma
        share.append((silu * up_value).astype(BF16))
        share.append((dhid * up_value * sigma * (1.0 + gate * (1.0 - sigma))).astype(BF16))
        share.append((dhid * silu).astype(BF16))
    share = jnp.stack(share).reshape(pair.shape)
    acts = lax.all_gather(share, "width_core", axis=0, tiled=False)
    hidden = acts[:, :, 0].reshape(units, slots)
    dgate = acts[:, :, 1].reshape(units, slots)
    dup = acts[:, :, 2].reshape(units, slots)

    place_x = lax.axis_index("hidden_x")
    sent, own = second_products(
        place_x.reshape(1), acts, gate_weight, up_weight, down_weight, size_x
    )
    sent = lax.all_to_all(
        sent.reshape(size_x, near, 8, width), "hidden_x", 0, 0, tiled=True
    )
    grad_gate = contract(flat_rows, dgate, 0, 1)
    grad_up = contract(flat_rows, dup, 0, 1)
    grad_down = contract(hidden, flat_cot, 1, 0)
    other = lax.broadcasted_iota(jnp.int32, (size_x, 1, 1, 1), 0) != place_x
    result = jnp.sum(jnp.where(other, sent.astype(F32), 0.0), axis=0)
    result = (own.reshape(near, 8, width) + result).astype(BF16)
    result = lax.all_to_all(result, NEAR, 0, 0, tiled=True)
    output, grad_rows = finish(labels, counts, result, mb)
    return (
        output.transpose(1, 0, 2),
        grad_rows.transpose(1, 0, 2),
        grad_gate[None],
        grad_up[None],
        grad_down[None],
    )


def solution(mesh):
    mesh = Mesh(mesh.devices.reshape((2,) + SUB), NAMES)
    owner_rows = P(None, OWNERS, WIDTH)
    return jax.shard_map(
        shards,
        mesh=mesh,
        in_specs=(
            owner_rows,
            owner_rows,
            P(None, OWNERS),
            P(None, OWNERS),
            P("branch", WIDTH, HIDDEN),
            P("branch", WIDTH, HIDDEN),
            P("branch", HIDDEN, WIDTH),
        ),
        out_specs=(
            owner_rows,
            owner_rows,
            P("branch", WIDTH, HIDDEN),
            P("branch", WIDTH, HIDDEN),
            P("branch", HIDDEN, WIDTH),
        ),
        check_vma=False,
    )
```

```python
import jax
import jax.numpy as jnp
from jax import lax
from jax.experimental import pallas as pl
from jax.experimental.pallas import tpu as pltpu
from jax.sharding import Mesh, PartitionSpec as P

CAP = 2
BF16 = jnp.bfloat16
F32 = jnp.float32
SUB = (4, 12, 4, 2)
NAMES = ("branch", "hidden_x", "hidden_z", "width_y", "width_core")
HIDDEN = ("hidden_x", "hidden_z")
WIDTH = ("width_y", "width_core")
OWNERS = ("branch",) + HIDDEN
NEAR = ("branch", "hidden_z")


def slot_picks(labels_ref, counts_ref, shape):
    row_dev = labels_ref.shape[1]
    lower = lax.broadcasted_iota(jnp.int32, shape, 0) == 0
    picks = [[[None] * row_dev for _ in range(CAP)] for _ in range(2)]
    for branch in range(2):
        slot = []
        for m in range(2):
            seen = jnp.int32(0)
            places = []
            for p in range(row_dev):
                chosen = (p < counts_ref[0, m]) & (labels_ref[m, p] == branch)
                places.append(jnp.where(chosen, seen, -1))
                seen = seen + jnp.where(chosen, 1, 0)
            slot.append(places)
        for p in range(row_dev):
            place = jnp.where(lower, slot[0][p], slot[1][p])
            for s in range(CAP):
                picks[branch][s][p] = place == s
    return picks


def pack_kernel(
    labels_in, counts_in, rows_in, cot_in, send_ref,
    labels_ref, counts_ref, rows_ref, cot_ref, scratch, sems,
):
    row_dev, mb, width = rows_ref.shape
    copies = [
        pltpu.make_async_copy(source, target, sems.at[i])
        for i, (source, target) in enumerate(
            (
                (labels_in, labels_ref),
                (counts_in, counts_ref),
                (rows_in, rows_ref),
                (cot_in, cot_ref),
            )
        )
    ]
    for copy in copies:
        copy.start()
    for copy in copies:
        copy.wait()
    picks = slot_picks(labels_ref, counts_ref, (mb, width))
    sources = [
        [ref[p].astype(F32) for p in range(row_dev)] for ref in (rows_ref, cot_ref)
    ]
    for branch in range(2):
        for which in range(2):
            for s in range(CAP):
                value = jnp.zeros((mb, width), F32)
                for p in range(row_dev):
                    value = jnp.where(picks[branch][s][p], sources[which][p], value)
                scratch[branch, pl.ds((which * CAP + s) * mb, mb), :] = value
        tile = scratch[branch].astype(BF16)
        for peer in range(send_ref.shape[1]):
            send_ref[branch, peer] = tile


def finish_kernel(labels_ref, counts_ref, recv_ref, out_ref, back_ref, scratch):
    row_dev, mb, width = out_ref.shape
    peers = recv_ref.shape[0] // 2
    picks = slot_picks(labels_ref, counts_ref, (mb, width))
    for branch in range(2):
        total = recv_ref[branch * peers].astype(F32)
        for peer in range(1, peers):
            total = total + recv_ref[branch * peers + peer].astype(F32)
        scratch[branch] = total
    for which, ref in enumerate((out_ref, back_ref)):
        for p in range(row_dev):
            value = jnp.zeros((mb, width), F32)
            for branch in range(2):
                for s in range(CAP):
                    value = jnp.where(
                        picks[branch][s][p],
                        scratch[branch, pl.ds((which * CAP + s) * mb, mb), :],
                        value,
                    )
            ref[p] = value.astype(BF16)


def first_kernel(core_ref, every_ref, gate_ref, up_ref, down_ref, mine_ref, theirs_ref):
    size_x, _, block, width = every_ref.shape
    size_y, _, share_units, slots = mine_ref.shape
    rows = every_ref[:, 0].reshape(slots, width)
    cot = every_ref[:, 1].reshape(slots, width)
    sums = (
        contract(gate_ref[...], rows, 0, 1),
        contract(up_ref[...], rows, 0, 1),
        contract(down_ref[...], cot, 1, 1),
    )
    for core in range(2):

        @pl.when(core_ref[0] == core)
        def _():
            for kind, total in enumerate(sums):
                for y in range(size_y):
                    for ref, c in ((mine_ref, core), (theirs_ref, 1 - core)):
                        start = (y * 2 + c) * share_units
                        ref[y, kind] = total[start : start + share_units]


def contract(left, right, left_dim, right_dim):
    return lax.dot_general(
        left, right, (((left_dim,), (right_dim,)), ((), ())), preferred_element_type=F32
    )


def own_kept(own, received, other):
    terms = jnp.where(other, received.astype(F32), own)
    total = terms[0]
    for i in range(1, terms.shape[0]):
        total = total + terms[i]
    return total


def full(shape):
    return pl.BlockSpec(shape, lambda: (0,) * len(shape))


def second_kernel(place_ref, acts_ref, gate_ref, up_ref, down_ref, sent_ref, own_ref, scratch):
    parts, kinds, share_units, slots = acts_ref.shape
    units = parts * share_units
    width = down_ref.shape[1]
    hidden = acts_ref[:, 0].reshape(units, slots)
    dgate = acts_ref[:, 1].reshape(units, slots)
    dup = acts_ref[:, 2].reshape(units, slots)
    out = contract(hidden, down_ref[...], 0, 0)
    back = contract(dgate, gate_ref[...], 0, 1) + contract(dup, up_ref[...], 0, 1)
    tiles = slots // 8
    out = out.reshape(tiles, 8, width)
    back = back.reshape(tiles, 8, width)
    first = lax.broadcasted_iota(jnp.int32, out.shape, 1) < 4
    even = jnp.where(first, out, pltpu.roll(back, 4, 1))
    odd = jnp.where(first, pltpu.roll(out, 4, 1), back)
    sent_ref[:, 0] = even.astype(BF16)
    sent_ref[:, 1] = odd.astype(BF16)
    scratch[:, 0] = even
    scratch[:, 1] = odd
    own_tiles = own_ref.shape[0]
    own_ref[...] = scratch[pl.ds(place_ref[0] * own_tiles, own_tiles)]


GRANT = pltpu.CompilerParams(vmem_limit_bytes=12 * 1024 * 1024)
SCALARS = pl.BlockSpec(memory_space=pltpu.SMEM)


def pack(labels, counts, rows, cotangent, peers):
    row_dev, mb, width = rows.shape
    shape = (2, peers, 2 * CAP * mb, width)
    return pl.pallas_call(
        pack_kernel,
        out_shape=jax.ShapeDtypeStruct(shape, BF16),
        in_specs=[pl.BlockSpec(memory_space=pltpu.HBM)] * 4,
        out_specs=full(shape),
        scratch_shapes=[
            pltpu.SMEM(labels.shape, jnp.int32),
            pltpu.SMEM(counts.shape, jnp.int32),
            pltpu.VMEM(rows.shape, BF16),
            pltpu.VMEM(rows.shape, BF16),
            pltpu.VMEM((2, 2 * CAP * mb, width), F32),
            pltpu.SemaphoreType.DMA((4,)),
        ],
        name="pack",
    )(labels, counts, rows, cotangent)


def finish(labels, counts, recv, mb):
    shape = (labels.shape[1], mb, recv.shape[2])
    return pl.pallas_call(
        finish_kernel,
        out_shape=(jax.ShapeDtypeStruct(shape, BF16),) * 2,
        in_specs=[SCALARS, SCALARS, full(recv.shape)],
        out_specs=(full(shape),) * 2,
        scratch_shapes=[pltpu.VMEM((2,) + recv.shape[1:], F32)],
        compiler_params=GRANT,
        name="finish",
    )(labels, counts, recv)


def first_products(core, every, gate_weight, up_weight, down_weight, size_y):
    units = gate_weight.shape[1]
    slots = every.shape[0] * every.shape[2]
    shape = (size_y, 3, units // (2 * size_y), slots)
    return pl.pallas_call(
        first_kernel,
        out_shape=(jax.ShapeDtypeStruct(shape, F32),) * 2,
        in_specs=[
            SCALARS,
            full(every.shape),
            full(gate_weight.shape),
            full(up_weight.shape),
            full(down_weight.shape),
        ],
        out_specs=(full(shape),) * 2,
        compiler_params=GRANT,
        name="first_products",
    )(core, every, gate_weight, up_weight, down_weight)


def second_products(place, acts, gate_weight, up_weight, down_weight, size_x):
    slots = acts.shape[3]
    width = down_weight.shape[1]
    shape = (slots // 8, 2, 8, width)
    own_shape = (slots // 8 // size_x, 2, 8, width)
    return pl.pallas_call(
        second_kernel,
        out_shape=(
            jax.ShapeDtypeStruct(shape, BF16),
            jax.ShapeDtypeStruct(own_shape, F32),
        ),
        in_specs=[
            pl.BlockSpec(memory_space=pltpu.SMEM),
            full(acts.shape),
            full(gate_weight.shape),
            full(up_weight.shape),
            full(down_weight.shape),
        ],
        out_specs=(full(shape), full(own_shape)),
        scratch_shapes=[pltpu.VMEM(shape, F32)],
        compiler_params=GRANT,
        name="second_products",
    )(place, acts, gate_weight, up_weight, down_weight)


def shards(rows, cotangent, labels, counts, gate_weight, up_weight, down_weight):
    gate_weight, up_weight, down_weight = gate_weight[0], up_weight[0], down_weight[0]
    mb, _, width = rows.shape
    size_x, size_z = lax.axis_size("hidden_x"), lax.axis_size("hidden_z")
    size_y, size_c = lax.axis_size("width_y"), lax.axis_size("width_core")
    near = 2 * size_z
    counts = counts.T
    per_owner = mb * CAP
    block = near * per_owner
    slots = size_x * block
    units = gate_weight.shape[1]

    send = pack(
        labels, counts, rows.transpose(1, 0, 2), cotangent.transpose(1, 0, 2), size_z
    )
    recv = lax.all_to_all(
        send.reshape(near, 2 * per_owner, width), NEAR, 0, 0, tiled=True
    )
    recv = recv.reshape(near, 2, per_owner, width).transpose(1, 0, 2, 3)
    every = lax.all_gather(recv.reshape(2, block, width), "hidden_x", axis=0, tiled=False)
    flat_rows = every[:, 0].reshape(slots, width)
    flat_cot = every[:, 1].reshape(slots, width)

    place_x = lax.axis_index("hidden_x")
    other_x = lax.broadcasted_iota(jnp.int32, (size_x, 1, 1), 0) != place_x
    other_y = lax.broadcasted_iota(jnp.int32, (size_y, 1, 1, 1), 0) != lax.axis_index(
        "width_y"
    )
    mine, theirs = first_products(
        lax.axis_index("width_core").reshape(1),
        every, gate_weight, up_weight, down_weight, size_y,
    )
    mine, theirs, other_x, other_y, place_x = lax.optimization_barrier(
        (mine, theirs, other_x, other_y, place_x)
    )
    pair = mine + lax.ppermute(theirs, "width_core", [(0, 1), (1, 0)])
    sent = lax.all_to_all(pair.astype(BF16), "width_y", 0, 0, tiled=True)
    gate, up_value, dhid = own_kept(pair, sent, other_y)
    sigma = jax.nn.sigmoid(gate)
    silu = gate * sigma
    share = jnp.stack(
        [
            (silu * up_value).astype(BF16),
            (dhid * up_value * sigma * (1.0 + gate * (1.0 - sigma))).astype(BF16),
            (dhid * silu).astype(BF16),
        ]
    )
    acts = lax.all_gather(share, WIDTH, axis=0, tiled=False)
    hidden = acts[:, 0].reshape(units, slots)
    dgate = acts[:, 1].reshape(units, slots)
    dup = acts[:, 2].reshape(units, slots)

    sent, own = second_products(
        place_x.reshape(1), acts, gate_weight, up_weight, down_weight, size_x
    )
    sent = lax.all_to_all(
        sent.reshape(size_x, near, 8, width), "hidden_x", 0, 0, tiled=True
    )
    grad_gate = contract(flat_rows, dgate, 0, 1)
    grad_up = contract(flat_rows, dup, 0, 1)
    grad_down = contract(hidden, flat_cot, 1, 0)
    result = own.reshape(near, 8, width)
    for i in range(size_x):
        result = result + jnp.where(other_x[i], sent[i].astype(F32), 0.0)
    result = result.astype(BF16)
    result = lax.all_to_all(result, NEAR, 0, 0, tiled=True)
    output, grad_rows = finish(labels, counts, result, mb)
    return (
        output.transpose(1, 0, 2),
        grad_rows.transpose(1, 0, 2),
        grad_gate[None],
        grad_up[None],
        grad_down[None],
    )


def solution(mesh):
    mesh = Mesh(mesh.devices.reshape((2,) + SUB), NAMES)
    owner_rows = P(None, OWNERS, WIDTH)
    return jax.shard_map(
        shards,
        mesh=mesh,
        in_specs=(
            owner_rows,
            owner_rows,
            P(None, OWNERS),
            P(None, OWNERS),
            P("branch", WIDTH, HIDDEN),
            P("branch", WIDTH, HIDDEN),
            P("branch", HIDDEN, WIDTH),
        ),
        out_specs=(
            owner_rows,
            owner_rows,
            P("branch", WIDTH, HIDDEN),
            P("branch", WIDTH, HIDDEN),
            P("branch", HIDDEN, WIDTH),
        ),
        check_vma=False,
    )
```

```python
import jax
import jax.numpy as jnp
from jax import lax
from jax.experimental import pallas as pl
from jax.experimental.pallas import tpu as pltpu
from jax.sharding import Mesh, PartitionSpec as P

CAP = 2
BF16 = jnp.bfloat16
F32 = jnp.float32
SUB = (4, 12, 4, 2)
NAMES = ("branch", "hidden_x", "hidden_z", "width_y", "width_core")
HIDDEN = ("hidden_x", "hidden_z")
WIDTH = ("width_y", "width_core")
OWNERS = ("branch",) + HIDDEN
NEAR = ("branch", "hidden_z")


def slot_picks(labels_ref, counts_ref, shape):
    row_dev = labels_ref.shape[1]
    lower = lax.broadcasted_iota(jnp.int32, shape, 0) == 0
    picks = [[[None] * row_dev for _ in range(CAP)] for _ in range(2)]
    for branch in range(2):
        slot = []
        for m in range(2):
            seen = jnp.int32(0)
            places = []
            for p in range(row_dev):
                chosen = (p < counts_ref[0, m]) & (labels_ref[m, p] == branch)
                places.append(jnp.where(chosen, seen, -1))
                seen = seen + jnp.where(chosen, 1, 0)
            slot.append(places)
        for p in range(row_dev):
            place = jnp.where(lower, slot[0][p], slot[1][p])
            for s in range(CAP):
                picks[branch][s][p] = place == s
    return picks


def pack_kernel(
    labels_in, counts_in, rows_in, cot_in, send_ref,
    labels_ref, counts_ref, rows_ref, cot_ref, scratch, sems,
):
    row_dev, mb, width = rows_ref.shape
    copies = [
        pltpu.make_async_copy(source, target, sems.at[i])
        for i, (source, target) in enumerate(
            (
                (labels_in, labels_ref),
                (counts_in, counts_ref),
                (rows_in, rows_ref),
                (cot_in, cot_ref),
            )
        )
    ]
    for copy in copies:
        copy.start()
    for copy in copies:
        copy.wait()
    picks = slot_picks(labels_ref, counts_ref, (mb, width))
    sources = [
        [ref[p].astype(F32) for p in range(row_dev)] for ref in (rows_ref, cot_ref)
    ]
    for branch in range(2):
        for which in range(2):
            for s in range(CAP):
                value = jnp.zeros((mb, width), F32)
                for p in range(row_dev):
                    value = jnp.where(picks[branch][s][p], sources[which][p], value)
                scratch[branch, pl.ds((which * CAP + s) * mb, mb), :] = value
        tile = scratch[branch].astype(BF16)
        for peer in range(send_ref.shape[1]):
            send_ref[branch, peer] = tile


def finish_kernel(labels_ref, counts_ref, recv_ref, out_ref, back_ref, scratch):
    row_dev, mb, width = out_ref.shape
    peers = recv_ref.shape[0] // 2
    picks = slot_picks(labels_ref, counts_ref, (mb, width))
    for branch in range(2):
        total = recv_ref[branch * peers].astype(F32)
        for peer in range(1, peers):
            total = total + recv_ref[branch * peers + peer].astype(F32)
        scratch[branch] = total
    for which, ref in enumerate((out_ref, back_ref)):
        for p in range(row_dev):
            value = jnp.zeros((mb, width), F32)
            for branch in range(2):
                for s in range(CAP):
                    value = jnp.where(
                        picks[branch][s][p],
                        scratch[branch, pl.ds((which * CAP + s) * mb, mb), :],
                        value,
                    )
            ref[p] = value.astype(BF16)


def first_kernel(core_ref, every_ref, gate_ref, up_ref, down_ref, mine_ref, theirs_ref):
    size_x, _, block, width = every_ref.shape
    size_y, _, share_units, slots = mine_ref.shape
    rows = every_ref[:, 0].reshape(slots, width)
    cot = every_ref[:, 1].reshape(slots, width)
    sums = (
        contract(gate_ref[...], rows, 0, 1),
        contract(up_ref[...], rows, 0, 1),
        contract(down_ref[...], cot, 1, 1),
    )
    for core in range(2):

        @pl.when(core_ref[0] == core)
        def _():
            for kind, total in enumerate(sums):
                for y in range(size_y):
                    for ref, c in ((mine_ref, core), (theirs_ref, 1 - core)):
                        start = (y * 2 + c) * share_units
                        ref[y, kind] = total[start : start + share_units]


def contract(left, right, left_dim, right_dim):
    return lax.dot_general(
        left, right, (((left_dim,), (right_dim,)), ((), ())), preferred_element_type=F32
    )


def own_kept(own, received, other):
    terms = jnp.where(other, received.astype(F32), own)
    total = terms[0]
    for i in range(1, terms.shape[0]):
        total = total + terms[i]
    return total


def full(shape):
    return pl.BlockSpec(shape, lambda: (0,) * len(shape))


def second_kernel(place_ref, acts_ref, gate_ref, up_ref, down_ref, sent_ref, own_ref, scratch):
    parts, kinds, share_units, slots = acts_ref.shape
    units = parts * share_units
    width = down_ref.shape[1]
    hidden = acts_ref[:, 0].reshape(units, slots)
    dgate = acts_ref[:, 1].reshape(units, slots)
    dup = acts_ref[:, 2].reshape(units, slots)
    out = contract(hidden, down_ref[...], 0, 0)
    back = contract(dgate, gate_ref[...], 0, 1) + contract(dup, up_ref[...], 0, 1)
    tiles = slots // 8
    out = out.reshape(tiles, 8, width)
    back = back.reshape(tiles, 8, width)
    first = lax.broadcasted_iota(jnp.int32, out.shape, 1) < 4
    even = jnp.where(first, out, pltpu.roll(back, 4, 1))
    odd = jnp.where(first, pltpu.roll(out, 4, 1), back)
    sent_ref[:, 0] = even.astype(BF16)
    sent_ref[:, 1] = odd.astype(BF16)
    scratch[:, 0] = even
    scratch[:, 1] = odd
    own_tiles = own_ref.shape[0]
    own_ref[...] = scratch[pl.ds(place_ref[0] * own_tiles, own_tiles)]


GRANT = pltpu.CompilerParams(vmem_limit_bytes=12 * 1024 * 1024)
SCALARS = pl.BlockSpec(memory_space=pltpu.SMEM)


def pack(labels, counts, rows, cotangent, peers):
    row_dev, mb, width = rows.shape
    shape = (2, peers, 2 * CAP * mb, width)
    return pl.pallas_call(
        pack_kernel,
        out_shape=jax.ShapeDtypeStruct(shape, BF16),
        in_specs=[pl.BlockSpec(memory_space=pltpu.HBM)] * 4,
        out_specs=full(shape),
        scratch_shapes=[
            pltpu.SMEM(labels.shape, jnp.int32),
            pltpu.SMEM(counts.shape, jnp.int32),
            pltpu.VMEM(rows.shape, BF16),
            pltpu.VMEM(rows.shape, BF16),
            pltpu.VMEM((2, 2 * CAP * mb, width), F32),
            pltpu.SemaphoreType.DMA((4,)),
        ],
        name="pack",
    )(labels, counts, rows, cotangent)


def finish(labels, counts, recv, mb):
    shape = (labels.shape[1], mb, recv.shape[2])
    return pl.pallas_call(
        finish_kernel,
        out_shape=(jax.ShapeDtypeStruct(shape, BF16),) * 2,
        in_specs=[SCALARS, SCALARS, full(recv.shape)],
        out_specs=(full(shape),) * 2,
        scratch_shapes=[pltpu.VMEM((2,) + recv.shape[1:], F32)],
        compiler_params=GRANT,
        name="finish",
    )(labels, counts, recv)


def first_products(core, every, gate_weight, up_weight, down_weight, size_y):
    units = gate_weight.shape[1]
    slots = every.shape[0] * every.shape[2]
    shape = (size_y, 3, units // (2 * size_y), slots)
    return pl.pallas_call(
        first_kernel,
        out_shape=(jax.ShapeDtypeStruct(shape, F32),) * 2,
        in_specs=[
            SCALARS,
            full(every.shape),
            full(gate_weight.shape),
            full(up_weight.shape),
            full(down_weight.shape),
        ],
        out_specs=(full(shape),) * 2,
        compiler_params=GRANT,
        name="first_products",
    )(core, every, gate_weight, up_weight, down_weight)


def second_products(place, acts, gate_weight, up_weight, down_weight, size_x):
    slots = acts.shape[3]
    width = down_weight.shape[1]
    shape = (slots // 8, 2, 8, width)
    own_shape = (slots // 8 // size_x, 2, 8, width)
    return pl.pallas_call(
        second_kernel,
        out_shape=(
            jax.ShapeDtypeStruct(shape, BF16),
            jax.ShapeDtypeStruct(own_shape, F32),
        ),
        in_specs=[
            pl.BlockSpec(memory_space=pltpu.SMEM),
            full(acts.shape),
            full(gate_weight.shape),
            full(up_weight.shape),
            full(down_weight.shape),
        ],
        out_specs=(full(shape), full(own_shape)),
        scratch_shapes=[pltpu.VMEM(shape, F32)],
        compiler_params=GRANT,
        name="second_products",
    )(place, acts, gate_weight, up_weight, down_weight)


def shards(rows, cotangent, labels, counts, gate_weight, up_weight, down_weight):
    gate_weight, up_weight, down_weight = gate_weight[0], up_weight[0], down_weight[0]
    mb, _, width = rows.shape
    size_x, size_z = lax.axis_size("hidden_x"), lax.axis_size("hidden_z")
    size_y, size_c = lax.axis_size("width_y"), lax.axis_size("width_core")
    near = 2 * size_z
    counts = counts.T
    per_owner = mb * CAP
    block = near * per_owner
    slots = size_x * block
    units = gate_weight.shape[1]

    send = pack(
        labels, counts, rows.transpose(1, 0, 2), cotangent.transpose(1, 0, 2), size_z
    )
    recv = lax.all_to_all(
        send.reshape(near, 2 * per_owner, width), NEAR, 0, 0, tiled=True
    )
    recv = recv.reshape(near, 2, per_owner, width).transpose(1, 0, 2, 3)
    every = lax.all_gather(recv.reshape(2, block, width), "hidden_x", axis=0, tiled=False)
    flat_rows = every[:, 0].reshape(slots, width)
    flat_cot = every[:, 1].reshape(slots, width)

    place_x = lax.axis_index("hidden_x")
    other_y = lax.broadcasted_iota(jnp.int32, (size_y, 1, 1, 1), 0) != lax.axis_index(
        "width_y"
    )
    mine, theirs = first_products(
        lax.axis_index("width_core").reshape(1),
        every, gate_weight, up_weight, down_weight, size_y,
    )
    mine, theirs, other_y, place_x = lax.optimization_barrier(
        (mine, theirs, other_y, place_x)
    )
    pair = mine + lax.ppermute(theirs, "width_core", [(0, 1), (1, 0)])
    sent = lax.all_to_all(pair.astype(BF16), "width_y", 0, 0, tiled=True)
    gate, up_value, dhid = own_kept(pair, sent, other_y)
    sigma = jax.nn.sigmoid(gate)
    silu = gate * sigma
    share = jnp.stack(
        [
            (silu * up_value).astype(BF16),
            (dhid * up_value * sigma * (1.0 + gate * (1.0 - sigma))).astype(BF16),
            (dhid * silu).astype(BF16),
        ]
    )
    acts = lax.all_gather(share, WIDTH, axis=0, tiled=False)
    hidden = acts[:, 0].reshape(units, slots)
    dgate = acts[:, 1].reshape(units, slots)
    dup = acts[:, 2].reshape(units, slots)

    sent, own = second_products(
        place_x.reshape(1), acts, gate_weight, up_weight, down_weight, size_x
    )
    sent = lax.all_to_all(
        sent.reshape(size_x, near, 8, width), "hidden_x", 0, 0, tiled=True
    )
    grad_gate = contract(flat_rows, dgate, 0, 1)
    grad_up = contract(flat_rows, dup, 0, 1)
    grad_down = contract(hidden, flat_cot, 1, 0)
    other = lax.broadcasted_iota(
        jnp.int32, (size_x, 1, 1, 1), 0
    ) != lax.axis_index("hidden_x")
    result = jnp.sum(jnp.where(other, sent.astype(F32), 0.0), axis=0)
    result = (own.reshape(near, 8, width) + result).astype(BF16)
    result = lax.all_to_all(result, NEAR, 0, 0, tiled=True)
    output, grad_rows = finish(labels, counts, result, mb)
    return (
        output.transpose(1, 0, 2),
        grad_rows.transpose(1, 0, 2),
        grad_gate[None],
        grad_up[None],
        grad_down[None],
    )


def solution(mesh):
    mesh = Mesh(mesh.devices.reshape((2,) + SUB), NAMES)
    owner_rows = P(None, OWNERS, WIDTH)
    return jax.shard_map(
        shards,
        mesh=mesh,
        in_specs=(
            owner_rows,
            owner_rows,
            P(None, OWNERS),
            P(None, OWNERS),
            P("branch", WIDTH, HIDDEN),
            P("branch", WIDTH, HIDDEN),
            P("branch", HIDDEN, WIDTH),
        ),
        out_specs=(
            owner_rows,
            owner_rows,
            P("branch", WIDTH, HIDDEN),
            P("branch", WIDTH, HIDDEN),
            P("branch", HIDDEN, WIDTH),
        ),
        check_vma=False,
    )
```

```python
import jax
import jax.numpy as jnp
from jax import lax
from jax.experimental import pallas as pl
from jax.experimental.pallas import tpu as pltpu
from jax.sharding import Mesh, PartitionSpec as P

CAP = 2
BF16 = jnp.bfloat16
F32 = jnp.float32
SUB = (4, 12, 4, 2)
NAMES = ("branch", "hidden_x", "hidden_z", "width_y", "width_core")
HIDDEN = ("hidden_x", "hidden_z")
WIDTH = ("width_y", "width_core")
OWNERS = ("branch",) + HIDDEN
NEAR = ("branch", "hidden_z")


def slot_picks(labels_ref, counts_ref, shape):
    row_dev = labels_ref.shape[1]
    lower = lax.broadcasted_iota(jnp.int32, shape, 0) == 0
    picks = [[[None] * row_dev for _ in range(CAP)] for _ in range(2)]
    for branch in range(2):
        slot = []
        for m in range(2):
            seen = jnp.int32(0)
            places = []
            for p in range(row_dev):
                chosen = (p < counts_ref[0, m]) & (labels_ref[m, p] == branch)
                places.append(jnp.where(chosen, seen, -1))
                seen = seen + jnp.where(chosen, 1, 0)
            slot.append(places)
        for p in range(row_dev):
            place = jnp.where(lower, slot[0][p], slot[1][p])
            for s in range(CAP):
                picks[branch][s][p] = place == s
    return picks


def pack_kernel(
    labels_in, counts_in, rows_in, cot_in, send_ref,
    labels_ref, counts_ref, rows_ref, cot_ref, scratch, sems,
):
    row_dev, mb, width = rows_ref.shape
    copies = [
        pltpu.make_async_copy(source, target, sems.at[i])
        for i, (source, target) in enumerate(
            (
                (labels_in, labels_ref),
                (counts_in, counts_ref),
                (rows_in, rows_ref),
                (cot_in, cot_ref),
            )
        )
    ]
    for copy in copies:
        copy.start()
    for copy in copies:
        copy.wait()
    picks = slot_picks(labels_ref, counts_ref, (mb, width))
    sources = [
        [ref[p].astype(F32) for p in range(row_dev)] for ref in (rows_ref, cot_ref)
    ]
    for branch in range(2):
        for which in range(2):
            for s in range(CAP):
                value = jnp.zeros((mb, width), F32)
                for p in range(row_dev):
                    value = jnp.where(picks[branch][s][p], sources[which][p], value)
                scratch[branch, pl.ds((which * CAP + s) * mb, mb), :] = value
        tile = scratch[branch].astype(BF16)
        for peer in range(send_ref.shape[1]):
            send_ref[branch, peer] = tile


def finish_kernel(labels_ref, counts_ref, recv_ref, out_ref, back_ref, scratch):
    row_dev, mb, width = out_ref.shape
    peers = recv_ref.shape[0] // 2
    picks = slot_picks(labels_ref, counts_ref, (mb, width))
    for branch in range(2):
        total = recv_ref[branch * peers].astype(F32)
        for peer in range(1, peers):
            total = total + recv_ref[branch * peers + peer].astype(F32)
        scratch[branch] = total
    for which, ref in enumerate((out_ref, back_ref)):
        for p in range(row_dev):
            value = jnp.zeros((mb, width), F32)
            for branch in range(2):
                for s in range(CAP):
                    value = jnp.where(
                        picks[branch][s][p],
                        scratch[branch, pl.ds((which * CAP + s) * mb, mb), :],
                        value,
                    )
            ref[p] = value.astype(BF16)


def first_kernel(core_ref, every_ref, gate_ref, up_ref, down_ref, mine_ref, theirs_ref):
    size_x, _, block, width = every_ref.shape
    pieces, _, piece_units, slots = mine_ref.shape
    rows = every_ref[:, 0].reshape(slots, width)
    cot = every_ref[:, 1].reshape(slots, width)
    sums = (
        contract(gate_ref[...], rows, 0, 1),
        contract(up_ref[...], rows, 0, 1),
        contract(down_ref[...], cot, 1, 1),
    )
    for core in range(2):

        @pl.when(core_ref[0] == core)
        def _():
            for kind, total in enumerate(sums):
                for piece in range(pieces):
                    for ref, c in ((mine_ref, core), (theirs_ref, 1 - core)):
                        start = (c * pieces + piece) * piece_units
                        ref[piece, kind] = total[start : start + piece_units]


def contract(left, right, left_dim, right_dim):
    return lax.dot_general(
        left, right, (((left_dim,), (right_dim,)), ((), ())), preferred_element_type=F32
    )


def full(shape):
    return pl.BlockSpec(shape, lambda: (0,) * len(shape))


def second_kernel(place_ref, acts_ref, gate_ref, up_ref, down_ref, sent_ref, own_ref, scratch):
    size_c, pieces, _, piece_units, slots = acts_ref.shape
    units = size_c * pieces * piece_units
    width = down_ref.shape[1]
    hidden = acts_ref[:, :, 0].reshape(units, slots)
    dgate = acts_ref[:, :, 1].reshape(units, slots)
    dup = acts_ref[:, :, 2].reshape(units, slots)
    out = contract(hidden, down_ref[...], 0, 0)
    back = contract(dgate, gate_ref[...], 0, 1) + contract(dup, up_ref[...], 0, 1)
    tiles = slots // 8
    out = out.reshape(tiles, 8, width)
    back = back.reshape(tiles, 8, width)
    first = lax.broadcasted_iota(jnp.int32, out.shape, 1) < 4
    even = jnp.where(first, out, pltpu.roll(back, 4, 1))
    odd = jnp.where(first, pltpu.roll(out, 4, 1), back)
    sent_ref[:, 0] = even.astype(BF16)
    sent_ref[:, 1] = odd.astype(BF16)
    scratch[:, 0] = even
    scratch[:, 1] = odd
    own_tiles = own_ref.shape[0]
    own_ref[...] = scratch[pl.ds(place_ref[0] * own_tiles, own_tiles)]


GRANT = pltpu.CompilerParams(vmem_limit_bytes=12 * 1024 * 1024)
SCALARS = pl.BlockSpec(memory_space=pltpu.SMEM)


def pack(labels, counts, rows, cotangent, peers):
    row_dev, mb, width = rows.shape
    shape = (2, peers, 2 * CAP * mb, width)
    return pl.pallas_call(
        pack_kernel,
        out_shape=jax.ShapeDtypeStruct(shape, BF16),
        in_specs=[pl.BlockSpec(memory_space=pltpu.HBM)] * 4,
        out_specs=full(shape),
        scratch_shapes=[
            pltpu.SMEM(labels.shape, jnp.int32),
            pltpu.SMEM(counts.shape, jnp.int32),
            pltpu.VMEM(rows.shape, BF16),
            pltpu.VMEM(rows.shape, BF16),
            pltpu.VMEM((2, 2 * CAP * mb, width), F32),
            pltpu.SemaphoreType.DMA((4,)),
        ],
        name="pack",
    )(labels, counts, rows, cotangent)


def finish(labels, counts, recv, mb):
    shape = (labels.shape[1], mb, recv.shape[2])
    return pl.pallas_call(
        finish_kernel,
        out_shape=(jax.ShapeDtypeStruct(shape, BF16),) * 2,
        in_specs=[SCALARS, SCALARS, full(recv.shape)],
        out_specs=(full(shape),) * 2,
        scratch_shapes=[pltpu.VMEM((2,) + recv.shape[1:], F32)],
        compiler_params=GRANT,
        name="finish",
    )(labels, counts, recv)


def first_products(core, every, gate_weight, up_weight, down_weight):
    units = gate_weight.shape[1]
    slots = every.shape[0] * every.shape[2]
    shape = (2, 3, units // 4, slots)
    return pl.pallas_call(
        first_kernel,
        out_shape=(jax.ShapeDtypeStruct(shape, F32),) * 2,
        in_specs=[
            SCALARS,
            full(every.shape),
            full(gate_weight.shape),
            full(up_weight.shape),
            full(down_weight.shape),
        ],
        out_specs=(full(shape),) * 2,
        compiler_params=GRANT,
        name="first_products",
    )(core, every, gate_weight, up_weight, down_weight)


def second_products(place, acts, gate_weight, up_weight, down_weight, size_x):
    slots = acts.shape[4]
    width = down_weight.shape[1]
    shape = (slots // 8, 2, 8, width)
    own_shape = (slots // 8 // size_x, 2, 8, width)
    return pl.pallas_call(
        second_kernel,
        out_shape=(
            jax.ShapeDtypeStruct(shape, BF16),
            jax.ShapeDtypeStruct(own_shape, F32),
        ),
        in_specs=[
            pl.BlockSpec(memory_space=pltpu.SMEM),
            full(acts.shape),
            full(gate_weight.shape),
            full(up_weight.shape),
            full(down_weight.shape),
        ],
        out_specs=(full(shape), full(own_shape)),
        scratch_shapes=[pltpu.VMEM(shape, F32)],
        compiler_params=GRANT,
        name="second_products",
    )(place, acts, gate_weight, up_weight, down_weight)


def shards(rows, cotangent, labels, counts, gate_weight, up_weight, down_weight):
    gate_weight, up_weight, down_weight = gate_weight[0], up_weight[0], down_weight[0]
    mb, _, width = rows.shape
    size_x, size_z = lax.axis_size("hidden_x"), lax.axis_size("hidden_z")
    size_y, size_c = lax.axis_size("width_y"), lax.axis_size("width_core")
    near = 2 * size_z
    counts = counts.T
    per_owner = mb * CAP
    block = near * per_owner
    slots = size_x * block
    units = gate_weight.shape[1]

    send = pack(
        labels, counts, rows.transpose(1, 0, 2), cotangent.transpose(1, 0, 2), size_z
    )
    recv = lax.all_to_all(
        send.reshape(near, 2 * per_owner, width), NEAR, 0, 0, tiled=True
    )
    recv = recv.reshape(near, 2, per_owner, width).transpose(1, 0, 2, 3)
    every = lax.all_gather(recv.reshape(2, block, width), "hidden_x", axis=0, tiled=False)
    flat_rows = every[:, 0].reshape(slots, width)
    flat_cot = every[:, 1].reshape(slots, width)

    mine, theirs = first_products(
        lax.axis_index("width_core").reshape(1),
        every, gate_weight, up_weight, down_weight,
    )
    pair = mine + lax.ppermute(theirs, "width_core", [(0, 1), (1, 0)])
    low = [(i, i ^ 1) for i in range(size_y)]
    high = [(i, (i + 1 if i % 2 else i - 1) % size_y) for i in range(size_y)]
    sums = [pair[0], pair[1]]
    for routes in ((low, high), (high, low)):
        sums = [
            own + lax.ppermute(own.astype(BF16), "width_y", route).astype(F32)
            for own, route in zip(sums, routes)
        ]
    share = []
    for gate, up_value, dhid in sums:
        sigma = jax.nn.sigmoid(gate)
        silu = gate * sigma
        share.append((silu * up_value).astype(BF16))
        share.append((dhid * up_value * sigma * (1.0 + gate * (1.0 - sigma))).astype(BF16))
        share.append((dhid * silu).astype(BF16))
    share = jnp.stack(share).reshape(pair.shape)
    acts = lax.all_gather(share, "width_core", axis=0, tiled=False)
    hidden = acts[:, :, 0].reshape(units, slots)
    dgate = acts[:, :, 1].reshape(units, slots)
    dup = acts[:, :, 2].reshape(units, slots)

    place_x = lax.axis_index("hidden_x")
    sent, own = second_products(
        place_x.reshape(1), acts, gate_weight, up_weight, down_weight, size_x
    )
    sent = lax.all_to_all(
        sent.reshape(size_x, near, 8, width), "hidden_x", 0, 0, tiled=True
    )
    grad_gate = contract(flat_rows, dgate, 0, 1)
    grad_up = contract(flat_rows, dup, 0, 1)
    grad_down = contract(hidden, flat_cot, 1, 0)
    other = lax.broadcasted_iota(jnp.int32, (size_x, 1, 1, 1), 0) != place_x
    result = jnp.sum(jnp.where(other, sent.astype(F32), 0.0), axis=0)
    result = (own.reshape(near, 8, width) + result).astype(BF16)
    result = lax.all_to_all(result, NEAR, 0, 0, tiled=True)
    output, grad_rows = finish(labels, counts, result, mb)
    return (
        output.transpose(1, 0, 2),
        grad_rows.transpose(1, 0, 2),
        grad_gate[None],
        grad_up[None],
        grad_down[None],
    )


def solution(mesh):
    mesh = Mesh(mesh.devices.reshape((2,) + SUB), NAMES)
    owner_rows = P(None, OWNERS, WIDTH)
    return jax.shard_map(
        shards,
        mesh=mesh,
        in_specs=(
            owner_rows,
            owner_rows,
            P(None, OWNERS),
            P(None, OWNERS),
            P("branch", WIDTH, HIDDEN),
            P("branch", WIDTH, HIDDEN),
            P("branch", HIDDEN, WIDTH),
        ),
        out_specs=(
            owner_rows,
            owner_rows,
            P("branch", WIDTH, HIDDEN),
            P("branch", WIDTH, HIDDEN),
            P("branch", HIDDEN, WIDTH),
        ),
        check_vma=False,
    )
```
